768 devices in a mesh: gx: 96 (over x, z, core), yz: 8 (over y).
Axes of the slice: x: 4, y: 8, z: 12, core: 2. Of those that a mesh axis runs over, the one named last changes fastest.
Arguments:
- populations: float32 [19, 768, 64, 128], P(None, 'gx', 'yz'), may hold values from 0.01 to 0.2
- solid: int32 [768, 64, 128], P('gx', 'yz'), may hold values 0 or 1
- displacement: float32 [3, 835584], P(None, ('gx', 'yz')), may hold values from -3 to 3
- stiffness: float32 [835584], P(('gx', 'yz')), may hold values from 0.05 to 0.5
- marker_tile: int32 [835584, 1], P(('gx', 'yz')), may hold values from 0 to 15, as said below
- marker_site: int32 [835584], P(('gx', 'yz')), may hold values from 0 to 8191
Outputs:
- final_populations: float32 [19, 768, 64, 128], P(None, 'gx', 'yz')
- final_displacement: float32 [3, 835584], P(None, ('gx', 'yz'))
The draws below stay inside these ranges and needn't reach their ends.
Inputs may be any that keep to these rules, and one draw needn't show every extreme that they name: `marker_tile`: among the rows of one device no value is named by more than 136 markers, and in every device's rows some value is named by exactly 136.
All inputs are finite; a program needn't handle non-finite values. No bound on the sum of `solid` on one device may be relied on, other than what follows from the above.
Results may differ from the reference program's by a relative error of at most 0.0003.
Values sent between devices are 32-bit elements; how exact they have to be, the bound alone decides.
A program may use at most 128 MiB of HBM per device.

```python
import math
import jax
import jax.numpy as jnp

CX = 8
CY = 8
CZ = 128
STEPS = 3
TILE_SLOTS = 16
MARK_DEV = 1088
MARKERS = 835584
SITES_DEV = 8192
CAP = 136
NX = 768
NY = 64
NZ = 128
N_GX = 96
N_YZ = 8


def device_tiles(device_key):
    pick_key, slot_key, order_key = jax.random.split(device_key, 3)
    fullest = jax.random.randint(pick_key, (), 0, TILE_SLOTS).astype(jnp.int32)
    chosen = jax.random.permutation(slot_key, (TILE_SLOTS - 1) * CAP)[:MARK_DEV - CAP].astype(jnp.int32)
    others = (fullest + 1 + chosen // CAP) % TILE_SLOTS
    filled = jnp.zeros((CAP,), jnp.int32) + fullest
    values = jnp.concatenate([filled, others.astype(jnp.int32)], axis=0)
    order = jax.random.permutation(order_key, MARK_DEV).astype(jnp.int32)
    return values[order]


def draw_marker_tile(key, part):
    devices_count = MARKERS // MARK_DEV
    device_keys = jax.random.split(jax.random.fold_in(key, 71), devices_count)
    values = jax.vmap(device_tiles)(device_keys)
    return values.reshape(-1, 1).astype(jnp.int32)


def set_ends(entries, key, smallest, high):
    extent = entries.shape
    index_at = [jax.random.randint(jax.random.fold_in(key, axis), (), 0, extent[axis]) for axis in range(len(extent))]
    entries = entries.at[tuple(index_at)].set(smallest)
    longest = extent.index(max(extent))
    index_at[longest] = (index_at[longest] + 1) % extent[longest]
    return entries.at[tuple(index_at)].set(high)


def level_of(stream_key, shape, cuts, smallest, largest):
    def one(dim, shards_of):
        draws = jax.random.uniform(jax.random.fold_in(jax.random.fold_in(stream_key, 6), dim), (shards_of,), jnp.float32, smallest / len(cuts), largest / len(cuts))
        return jnp.repeat(jnp.exp(draws), shape[dim] // shards_of).reshape((-1,) + (1,) * (len(shape) - dim - 1))

    factor_of = one(*cuts[0])
    for cut in cuts[1:]:
        factor_of = factor_of * one(*cut)
    return factor_of


def scatter_about(key, dims, scale, most, cuts=(), held_as=jnp.bfloat16):
    values = jax.random.normal(key, dims, jnp.float32) * scale
    if len(cuts) > 0:
        values = level_of(key, dims, cuts, -0.22, 0.18) * values
    return jnp.clip(values, min=-most, max=most).astype(held_as)


def setup_inputs(seed: int = 0) -> dict:
    key_list = jax.random.split(jax.random.key(seed), 7)
    populations = jnp.clip(0.01 + 0.19 * jax.random.uniform(key_list[0], (19, NX, NY, NZ), jnp.float32) ** level_of(key_list[0], (19, NX, NY, NZ), ((1, 96), (2, 8)), -0.2, 0.2), 0.01, 0.2)
    solid = set_ends((jax.random.randint(key_list[1], (NX, NY, NZ), 0, 8) < 1).astype(jnp.int32), jax.random.fold_in(key_list[1], 1), 0, 1)
    displacement = scatter_about(key_list[2], (3, MARKERS), 0.5, 3.0, ((1, 768),), jnp.float32)
    stiffness = jnp.clip(jnp.exp(math.log(0.5) - 2.3025851 * jax.random.uniform(key_list[3], (MARKERS,), jnp.float32) ** level_of(key_list[3], (MARKERS,), ((0, 768),), -0.2, 0.2)), 0.05, 0.5)
    marker_tile = draw_marker_tile(jax.random.fold_in(key_list[6], 71), 0)
    marker_site = set_ends(jax.random.randint(key_list[5], (MARKERS,), 0, SITES_DEV), jax.random.fold_in(key_list[5], 1), 0, SITES_DEV - 1).astype(jnp.int32)
    return {"populations": populations, "solid": solid, "displacement": displacement, "stiffness": stiffness, "marker_tile": marker_tile, "marker_site": marker_site}


lattice_dirs = [(0, 0, 0), (1, 0, 0), (-1, 0, 0), (0, 1, 0), (0, -1, 0), (0, 0, 1), (0, 0, -1),
                (1, 1, 0), (-1, -1, 0), (1, -1, 0), (-1, 1, 0),
                (1, 0, 1), (-1, 0, -1), (1, 0, -1), (-1, 0, 1),
                (0, 1, 1), (0, -1, -1), (0, 1, -1), (0, -1, 1)]
lattice_weights = [1.0 / 3.0] + [1.0 / 18.0] * 6 + [1.0 / 36.0] * 12
opposite_dirs = [0, 2, 1, 4, 3, 6, 5, 8, 7, 10, 9, 12, 11, 14, 13, 16, 15, 18, 17]
relax_rate = 1.6


def weighted(offsets, parts, blank):
    total = blank
    for component in range(3):
        if offsets[component] != 0:
            total = total + offsets[component] * parts[component]
    return total


def collide(popul, field, solid):
    density = jnp.sum(popul, axis=0)
    moments = []
    for component in range(3):
        total = 0.5 * field[component]
        for index in range(19):
            offset = lattice_dirs[index][component]
            if offset != 0:
                total = total + offset * popul[index]
        moments.append(total / density)
    squared = moments[0] * moments[0] + moments[1] * moments[1] + moments[2] * moments[2]
    speed_field = moments[0] * field[0] + moments[1] * field[1] + moments[2] * field[2]
    blank = jnp.zeros_like(density)
    result = []
    for index in range(19):
        offsets = lattice_dirs[index]
        weight = lattice_weights[index]
        along = weighted(offsets, moments, blank)
        pushed = weighted(offsets, field, blank)
        drift = pushed - speed_field
        equil = weight * density * (1.0 + 3.0 * along + 4.5 * along * along - 1.5 * squared)
        source = (1.0 - 0.5 * relax_rate) * weight * (3.0 * drift + 9.0 * along * pushed)
        post = popul[index] - relax_rate * (popul[index] - equil) + source
        result.append(jnp.where(solid == 1, popul[opposite_dirs[index]], post))
    return jnp.stack(result), jnp.stack(moments)


def reference(populations, solid, displacement, stiffness, marker_tile, marker_site):
    total_rows = displacement.shape[1]
    rows = jnp.arange(total_rows, dtype=jnp.int32)
    owner = rows // MARK_DEV
    owner_x = owner // N_YZ
    value = marker_tile[:, 0]
    tile_x = (owner_x + value // N_YZ) % N_GX
    tile_y = value % N_YZ
    xs = tile_x * CX + marker_site // (CY * CZ)
    ys = tile_y * CY + (marker_site // CZ) % CY
    zs = marker_site % CZ
    flat = ((xs * NY + ys) * NZ + zs).astype(jnp.int32)
    popul = populations
    moved = displacement
    for step in range(STEPS):
        force = -stiffness[None, :] * moved
        field = jnp.zeros((3, NX * NY * NZ), jnp.float32).at[:, flat].add(force)
        field = field.reshape(3, NX, NY, NZ)
        post, speed = collide(popul, field, solid)
        moved = moved + speed.reshape(3, -1)[:, flat]
        popul = jnp.stack([jnp.roll(post[index], lattice_dirs[index], axis=(0, 1, 2)) for index in range(19)])
    return popul, moved
```

```python
import functools

import jax
import jax.numpy as jnp
from jax import lax
from jax.experimental import pallas as pl
from jax.experimental.pallas import tpu as pltpu
from jax.sharding import PartitionSpec as P

MESH = pl.DeviceIdType.MESH
STEPS = 3
F32 = jnp.float32
BF16 = jnp.bfloat16
I32 = jnp.int32

lattice_dirs = [
    (0, 0, 0),
    (1, 0, 0),
    (-1, 0, 0),
    (0, 1, 0),
    (0, -1, 0),
    (0, 0, 1),
    (0, 0, -1),
    (1, 1, 0),
    (-1, -1, 0),
    (1, -1, 0),
    (-1, 1, 0),
    (1, 0, 1),
    (-1, 0, -1),
    (1, 0, -1),
    (-1, 0, 1),
    (0, 1, 1),
    (0, -1, -1),
    (0, 1, -1),
    (0, -1, 1),
]
lattice_weights = [1.0 / 3.0] + [1.0 / 18.0] * 6 + [1.0 / 36.0] * 12
relax_rate = 1.6
PUSH = 1.0 - 0.5 * relax_rate

X_FACE = [[1, 7, 9, 11, 13], [2, 8, 10, 12, 14]]
Y_FACE = [[3, 7, 10, 15, 17], [4, 8, 9, 16, 18]]
CORNER = [7, 8, 9, 10]

YZ = 8
TILES = 2 * YZ
LANES = 128
GROUPS = TILES + 1
SLOTS = GROUPS * LANES
BIN_PARTS = 3
STEP_PARTS = 2


def parts_of(value, count):
    parts = []
    rest = value
    for _ in range(count):
        part = rest.astype(BF16).astype(F32)
        parts.append(part)
        rest = rest - part
    return parts


def iota(shape, dim):
    return lax.broadcasted_iota(I32, shape, dim)


def spread(value):
    for shift in (8, 16, 32, 64):
        value = value + pltpu.roll(value, shift, 1)
    return value


def product(lhs, rhs, transposed):
    dims = (((1,), (1 if transposed else 0,)), ((), ()))
    return lax.dot_general(lhs, rhs, dims, preferred_element_type=F32)


def collide(popul, field, solid):
    density = popul[0]
    for index in range(1, 19):
        density = density + popul[index]
    moved = []
    for component in range(3):
        total = 0.5 * field[component]
        for index in range(1, 19, 2):
            offset = lattice_dirs[index][component]
            if offset > 0:
                total = total + (popul[index] - popul[index + 1])
            elif offset < 0:
                total = total - (popul[index] - popul[index + 1])
        moved.append(total)
    inverse = 1.0 / density
    speed = [total * inverse for total in moved]
    squared = speed[0] * speed[0] + speed[1] * speed[1] + speed[2] * speed[2]
    speed_field = speed[0] * field[0] + speed[1] * field[1] + speed[2] * field[2]
    dense = relax_rate * density
    base = dense - 1.5 * dense * squared - (3.0 * PUSH) * speed_field
    even = [(4.5 * relax_rate) * moved[c] + (9.0 * PUSH) * field[c] for c in range(3)]
    odd = [(3.0 * relax_rate) * moved[c] + (3.0 * PUSH) * field[c] for c in range(3)]
    wall = solid == 1
    keep = 1.0 - relax_rate
    result = [None] * 19
    result[0] = jnp.where(wall, popul[0], keep * popul[0] + lattice_weights[0] * base)

    def along(offsets, values):
        total = None
        for component in range(3):
            if offsets[component] != 0:
                term = values[component]
                if total is None:
                    total = term if offsets[component] > 0 else -term
                else:
                    total = total + term if offsets[component] > 0 else total - term
        return total

    for index in range(1, 19, 2):
        offsets = lattice_dirs[index]
        weight = lattice_weights[index]
        both = weight * (base + along(offsets, speed) * along(offsets, even))
        side = weight * along(offsets, odd)
        result[index] = jnp.where(wall, popul[index + 1], keep * popul[index] + (both + side))
        result[index + 1] = jnp.where(wall, popul[index], keep * popul[index + 1] + (both - side))
    return result, speed


def kernel(
    pop_hbm, solid_hbm, disp_ref, stiff_ref, tile_ref, site_ref,
    out_ref, dout_ref,
    start, solid, vals, tiles, hot, payload, recv, zhot, lhs, ubuf, field, slots,
    post, sx, sy, rx, ry, rc, back, ret,
    load_sem, put_send, put_recv, ret_send, ret_recv, halo_send, halo_recv,
):
    marks = disp_ref.shape[1]
    wide = vals.shape[1]
    blocks = wide // LANES
    n_gx = lax.axis_size("gx")
    g = lax.axis_index("gx")
    q = lax.axis_index("yz")

    def device(dg, dq):
        return (lax.rem(g + (dg + n_gx), n_gx), lax.rem(q + (dq + YZ), YZ))

    barrier = pltpu.get_barrier_semaphore()
    for dg in (-1, 0, 1):
        for dq in range(YZ):
            if (dg, dq) != (0, 0):
                pl.semaphore_signal(barrier, inc=1, device_id=device(dg, dq), device_id_type=MESH)

    load_pop = pltpu.make_async_copy(pop_hbm, start, load_sem.at[0])
    load_solid = pltpu.make_async_copy(solid_hbm, solid, load_sem.at[1])
    load_pop.start()
    load_solid.start()

    sub = iota((8, LANES), 0)
    lane_group = iota((8, LANES), 1) // 8
    own_group = lane_group == sub

    vals[...] = jnp.zeros_like(vals)
    tiles[...] = jnp.full_like(tiles, -1)
    tile = tile_ref[...]
    tiles[0:1, 0:marks] = (tile & YZ) + ((tile - q) & (YZ - 1))
    vals[0:1, 0:marks] = site_ref[...].astype(F32)
    vals[1:2, 0:marks] = stiff_ref[...]
    vals[2:5, 0:marks] = disp_ref[...]
    member = iota((TILES, wide), 0) == tiles[0:1, :]
    member_f = jnp.where(member, 1.0, 0.0)
    stacked = jnp.concatenate([member_f[:, b * LANES : (b + 1) * LANES] for b in range(blocks)], axis=0)
    upper = jnp.where(iota((LANES, LANES), 0) <= iota((LANES, LANES), 1), 1.0, 0.0).astype(BF16)
    counts = product(stacked.astype(BF16), upper, False)
    offset = jnp.full((TILES, 1), -1.0, F32)
    ranks = []
    for b in range(blocks):
        count = counts[b * TILES : (b + 1) * TILES, :]
        mine = member_f[:, b * LANES : (b + 1) * LANES]
        ranks.append(jnp.sum(mine * (count + offset), axis=0, keepdims=True))
        offset = offset + count[:, LANES - 1 : LANES]
    rank = jnp.concatenate(ranks, axis=1).astype(I32)
    row = iota((2 * LANES, wide), 0)
    wanted = jnp.where(row < LANES, row, LANES + (row & 7))
    hot[...] = jnp.where(wanted == rank, 1.0, 0.0).astype(BF16)

    binned = None
    for part in parts_of(vals[...], BIN_PARTS):
        left = jnp.concatenate(
            [jnp.where(member[k : k + 1, :], part, 0.0) for k in range(TILES)], axis=0
        ).astype(BF16)
        term = product(left, hot[...], True)
        binned = term if binned is None else binned + term
    for k in range(TILES):
        main = binned[k * 8 : (k + 1) * 8, 0:LANES]
        more = binned[k * 8 : (k + 1) * 8, LANES : 2 * LANES]
        more = jnp.sum(jnp.where(own_group, more, 0.0), axis=0, keepdims=True)
        payload[k] = jnp.where(sub == 5, more, main)

    pl.semaphore_wait(barrier, 3 * YZ - 1)

    puts = []
    for k in reversed(range(1, TILES)):
        put = pltpu.make_async_remote_copy(
            src_ref=payload.at[k],
            dst_ref=recv.at[k],
            send_sem=put_send.at[k],
            recv_sem=put_recv.at[k],
            device_id=device(k // YZ, k % YZ),
            device_id_type=MESH,
        )
        put.start()
        puts.append(put)
    load_pop.wait()
    load_solid.wait()
    for put in puts:
        put.wait_recv()

    tail = jnp.zeros((8, LANES), F32)
    for k in range(TILES):
        block = payload[0] if k == 0 else recv[k]
        slots[k] = block
        more = jnp.where(own_group, jnp.broadcast_to(block[5:6, :], (8, LANES)), 0.0)
        tail = tail + jnp.where(lane_group == k, spread(more), 0.0)
    slots[TILES] = tail
    rows32 = iota((32, LANES), 0)
    for k in range(GROUPS):
        site = slots[k][0:1, :].astype(I32)
        place = ((site >> 12) << 7) + (site & 127)
        zhot[:, k * LANES : (k + 1) * LANES] = jnp.where(
            iota((2 * LANES, LANES), 0) == place, 1.0, 0.0
        ).astype(BF16)

    def row_mask(block):
        return rows32 == ((block[0:1, :].astype(I32) >> 7) & 31)

    def deposit():
        for k in range(GROUPS):
            block = slots[k]
            mask = row_mask(block)
            force = -block[1:2, :] * block
            for number, part in enumerate(parts_of(force, STEP_PARTS)):
                for c in range(3):
                    top = number * 96 + c * 32
                    lhs[top : top + 32, k * LANES : (k + 1) * LANES] = jnp.where(
                        mask, part[2 + c : 3 + c, :], 0.0
                    ).astype(BF16)
        result = product(lhs[...], zhot[...], True)
        total = result[0:96, :]
        for number in range(1, STEP_PARTS):
            total = total + result[number * 96 : (number + 1) * 96, :]
        field[...] = total

    def gather():
        left = jnp.concatenate([part.astype(BF16) for part in parts_of(ubuf[...], STEP_PARTS)], axis=0)
        for k in range(GROUPS):
            block = slots[k]
            mask = row_mask(block)
            picked = product(left, zhot[:, k * LANES : (k + 1) * LANES], False)
            total = picked[0:96, :]
            for number in range(1, STEP_PARTS):
                total = total + picked[number * 96 : (number + 1) * 96, :]
            for c in range(3):
                speed = jnp.sum(
                    jnp.where(mask, total[c * 32 : (c + 1) * 32, :], 0.0), axis=0, keepdims=True
                )
                block = block + jnp.where(sub == 2 + c, speed, 0.0)
            slots[k] = block

    def pulled(step, index, a):
        cx, cy, cz = lattice_dirs[index]
        x_side = 0 if cx > 0 else 1
        y_side = 0 if cy > 0 else 1
        source = a - cx
        inside = 0 <= source < 8
        if inside:
            value = post[step % 2, index, source]
        else:
            value = rx[step, x_side, X_FACE[x_side].index(index)]
        if cy != 0:
            if inside:
                other = jnp.broadcast_to(
                    ry[step, y_side, Y_FACE[y_side].index(index), source : source + 1, :], (8, LANES)
                )
            else:
                other = rc[step, CORNER.index(index)]
            value = jnp.where(sub == (7 if cy > 0 else 0), other, value)
            value = pltpu.roll(value, cy % 8, 0)
        if cz != 0:
            value = pltpu.roll(value, cz % LANES, 1)
        return value

    def halo(step, which, src, dst, dg, dq):
        return pltpu.make_async_remote_copy(
            src_ref=src,
            dst_ref=dst,
            send_sem=halo_send.at[step * 8 + which],
            recv_sem=halo_recv.at[step * 8 + which],
            device_id=device(dg, dq),
            device_id_type=MESH,
        )

    def slice_step(step, a):
        if step == 0:
            popul = [start[index, a] for index in range(19)]
        else:
            popul = [pulled(step - 1, index, a) for index in range(19)]
        low = (a % 4) * 8
        high = (a // 4) * LANES
        fields = [field[c * 32 + low : c * 32 + low + 8, high : high + LANES] for c in range(3)]
        result, speed = collide(popul, fields, solid[a])
        for c in range(3):
            ubuf[c * 32 + low : c * 32 + low + 8, high : high + LANES] = speed[c]
        for index in range(19):
            post[step % 2, index, a] = result[index]
        for side, edge in ((0, 7), (1, 0)):
            if a == edge:
                for place, index in enumerate(X_FACE[side]):
                    sx[step, side, place] = result[index]
            for place, index in enumerate(Y_FACE[side]):
                sy[step, side, place, a : a + 1, :] = result[index][edge : edge + 1, :]

    returns = []
    sent = []
    deposit()
    for step in range(STEPS):
        copies = []
        slice_step(step, 0)
        slice_step(step, 7)
        for number, index in enumerate(CORNER):
            cx, cy, _ = lattice_dirs[index]
            side = 0 if cx > 0 else 1
            copies.append(
                halo(step, number, sx.at[step, side, X_FACE[side].index(index)], rc.at[step, number], cx, cy)
            )
            copies[-1].start()
        for side, dg in ((0, 1), (1, -1)):
            copies.append(halo(step, 4 + side, sx.at[step, side], rx.at[step, side], dg, 0))
            copies[-1].start()
        for a in range(1, 7):
            slice_step(step, a)
        for side, dq in ((0, 1), (1, -1)):
            copies.append(halo(step, 6 + side, sy.at[step, side], ry.at[step, side], 0, dq))
            copies[-1].start()
        gather()
        if step < STEPS - 1:
            deposit()
        else:
            tail = slots[TILES]
            for k in reversed(range(TILES)):
                more = spread(jnp.where(lane_group == k, tail, 0.0))
                more = jnp.sum(jnp.where(own_group, more, 0.0), axis=0, keepdims=True)
                block = jnp.where(sub == 5, more, slots[k])
                if k == 0:
                    ret[0] = block
                else:
                    back[k] = block
                    copy = pltpu.make_async_remote_copy(
                        src_ref=back.at[k],
                        dst_ref=ret.at[k],
                        send_sem=ret_send.at[k],
                        recv_sem=ret_recv.at[k],
                        device_id=device(-(k // YZ), -(k % YZ)),
                        device_id_type=MESH,
                    )
                    copy.start()
                    returns.append(copy)
        for copy in copies:
            copy.wait_recv()
        sent.extend(copies)

    for a in range(8):
        for index in range(19):
            out_ref[index, a] = pulled(STEPS - 1, index, a)

    for copy in returns:
        copy.wait_recv()
    lefts = []
    for k in range(TILES):
        block = ret[k]
        more = jnp.where(own_group, jnp.broadcast_to(block[5:6, :], (8, LANES)), 0.0)
        lefts.append(jnp.concatenate([block, more], axis=1))
    left = jnp.concatenate(lefts, axis=0)
    taken = None
    for part in parts_of(left, BIN_PARTS):
        term = product(part.astype(BF16), hot[...], False)
        taken = term if taken is None else taken + term
    member = iota((TILES, wide), 0) == tiles[0:1, :]
    final = None
    for k in range(TILES):
        term = jnp.where(member[k : k + 1, :], taken[k * 8 : (k + 1) * 8, :], 0.0)
        final = term if final is None else final + term
    dout_ref[...] = final[2:5, 0:marks]
    for copy in puts + sent + returns:
        copy.wait_send()


def body(populations, solid, displacement, stiffness, marker_tile, marker_site):
    marks = displacement.shape[1]
    wide = -(-marks // LANES) * LANES
    vmem = pl.BlockSpec(memory_space=pltpu.VMEM)
    hbm = pl.BlockSpec(memory_space=pl.ANY)
    dma = pltpu.SemaphoreType.DMA
    return pl.pallas_call(
        kernel,
        out_shape=(
            jax.ShapeDtypeStruct(populations.shape, F32),
            jax.ShapeDtypeStruct(displacement.shape, F32),
        ),
        in_specs=[hbm, hbm, vmem, vmem, vmem, vmem],
        out_specs=(vmem, vmem),
        scratch_shapes=[
            pltpu.VMEM(populations.shape, F32),
            pltpu.VMEM(solid.shape, I32),
            pltpu.VMEM((8, wide), F32),
            pltpu.VMEM((8, wide), I32),
            pltpu.VMEM((2 * LANES, wide), BF16),
            pltpu.VMEM((TILES, 8, LANES), F32),
            pltpu.VMEM((TILES, 8, LANES), F32),
            pltpu.VMEM((2 * LANES, SLOTS), BF16),
            pltpu.VMEM((96 * STEP_PARTS, SLOTS), BF16),
            pltpu.VMEM((96, 2 * LANES), F32),
            pltpu.VMEM((96, 2 * LANES), F32),
            pltpu.VMEM((GROUPS, 8, LANES), F32),
            pltpu.VMEM((2,) + populations.shape, F32),
            pltpu.VMEM((STEPS, 2, 5, 8, LANES), F32),
            pltpu.VMEM((STEPS, 2, 5, 8, LANES), F32),
            pltpu.VMEM((STEPS, 2, 5, 8, LANES), F32),
            pltpu.VMEM((STEPS, 2, 5, 8, LANES), F32),
            pltpu.VMEM((STEPS, 4, 8, LANES), F32),
            pltpu.VMEM((TILES, 8, LANES), F32),
            pltpu.VMEM((TILES, 8, LANES), F32),
            dma((2,)),
            dma((TILES,)),
            dma((TILES,)),
            dma((TILES,)),
            dma((TILES,)),
            dma((STEPS * 8,)),
            dma((STEPS * 8,)),
        ],
        compiler_params=pltpu.CompilerParams(collective_id=0, has_side_effects=True),
        name="lattice_steps",
    )(
        populations,
        solid,
        displacement,
        stiffness.reshape(1, -1),
        marker_tile.reshape(1, -1),
        marker_site.reshape(1, -1),
    )


def solution(mesh):
    in_specs = (
        P(None, "gx", "yz", None),
        P("gx", "yz", None),
        P(None, ("gx", "yz")),
        P(("gx", "yz")),
        P(("gx", "yz"), None),
        P(("gx", "yz")),
    )
    out_specs = (P(None, "gx", "yz", None), P(None, ("gx", "yz")))
    return jax.shard_map(body, mesh=mesh, in_specs=in_specs, out_specs=out_specs, check_vma=False)
```

```python
import functools

import jax
import jax.numpy as jnp
from jax import lax
from jax.experimental import pallas as pl
from jax.experimental.pallas import tpu as pltpu
from jax.sharding import PartitionSpec as P

MESH = pl.DeviceIdType.MESH
STEPS = 3
F32 = jnp.float32
BF16 = jnp.bfloat16
I32 = jnp.int32

lattice_dirs = [
    (0, 0, 0),
    (1, 0, 0),
    (-1, 0, 0),
    (0, 1, 0),
    (0, -1, 0),
    (0, 0, 1),
    (0, 0, -1),
    (1, 1, 0),
    (-1, -1, 0),
    (1, -1, 0),
    (-1, 1, 0),
    (1, 0, 1),
    (-1, 0, -1),
    (1, 0, -1),
    (-1, 0, 1),
    (0, 1, 1),
    (0, -1, -1),
    (0, 1, -1),
    (0, -1, 1),
]
lattice_weights = [1.0 / 3.0] + [1.0 / 18.0] * 6 + [1.0 / 36.0] * 12
relax_rate = 1.6
PUSH = 1.0 - 0.5 * relax_rate

X_FACE = [[1, 7, 9, 11, 13], [2, 8, 10, 12, 14]]
Y_FACE = [[3, 7, 10, 15, 17], [4, 8, 9, 16, 18]]
CORNER = [7, 8, 9, 10]

YZ = 8
TILES = 2 * YZ
LANES = 128
GROUPS = TILES + 1
SLOTS = GROUPS * LANES
BIN_PARTS = 2
PUT_ROWS = 6
STEP_PARTS = 2


def parts_of(value, count):
    parts = []
    rest = value
    for _ in range(count):
        part = rest.astype(BF16).astype(F32)
        parts.append(part)
        rest = rest - part
    return parts


def iota(shape, dim):
    return lax.broadcasted_iota(I32, shape, dim)


def spread(value):
    for shift in (8, 16, 32, 64):
        value = value + pltpu.roll(value, shift, 1)
    return value


def product(lhs, rhs, transposed):
    dims = (((1,), (1 if transposed else 0,)), ((), ()))
    return lax.dot_general(lhs, rhs, dims, preferred_element_type=F32)


def collide(popul, field, solid):
    density = popul[0]
    for index in range(1, 19):
        density = density + popul[index]
    moved = []
    for component in range(3):
        total = 0.5 * field[component]
        for index in range(1, 19, 2):
            offset = lattice_dirs[index][component]
            if offset > 0:
                total = total + (popul[index] - popul[index + 1])
            elif offset < 0:
                total = total - (popul[index] - popul[index + 1])
        moved.append(total)
    inverse = 1.0 / density
    speed = [total * inverse for total in moved]
    squared = speed[0] * speed[0] + speed[1] * speed[1] + speed[2] * speed[2]
    speed_field = speed[0] * field[0] + speed[1] * field[1] + speed[2] * field[2]
    dense = relax_rate * density
    base = dense - 1.5 * dense * squared - (3.0 * PUSH) * speed_field
    even = [(4.5 * relax_rate) * moved[c] + (9.0 * PUSH) * field[c] for c in range(3)]
    odd = [(3.0 * relax_rate) * moved[c] + (3.0 * PUSH) * field[c] for c in range(3)]
    wall = solid == 1
    keep = 1.0 - relax_rate
    result = [None] * 19
    result[0] = jnp.where(wall, popul[0], keep * popul[0] + lattice_weights[0] * base)

    def along(offsets, values):
        total = None
        for component in range(3):
            if offsets[component] != 0:
                term = values[component]
                if total is None:
                    total = term if offsets[component] > 0 else -term
                else:
                    total = total + term if offsets[component] > 0 else total - term
        return total

    for index in range(1, 19, 2):
        offsets = lattice_dirs[index]
        weight = lattice_weights[index]
        both = weight * (base + along(offsets, speed) * along(offsets, even))
        side = weight * along(offsets, odd)
        result[index] = jnp.where(wall, popul[index + 1], keep * popul[index] + (both + side))
        result[index + 1] = jnp.where(wall, popul[index], keep * popul[index + 1] + (both - side))
    return result, speed


def kernel(
    pop_hbm, solid_hbm, disp_hbm, stiff_hbm, tile_hbm, site_hbm,
    out_ref, dout_ref,
    start, solid, disp, stiff, tile_in, site_in, vals, hot, payload, recv, zhot, lhs, usum, field, slots,
    post, edges, halos, back, ret,
    load_sem, put_send, put_recv, ret_send, ret_recv, halo_send, halo_recv,
):
    marks = disp_hbm.shape[1]
    wide = vals.shape[1]
    blocks = wide // LANES
    n_gx = lax.axis_size("gx")
    g = lax.axis_index("gx")
    q = lax.axis_index("yz")
    g_of = {0: g, 1: lax.rem(g + 1, n_gx), -1: lax.rem(g + (n_gx - 1), n_gx)}
    q_of = [q if dq == 0 else (q + dq) & (YZ - 1) for dq in range(YZ)]

    def device(dg, dq):
        return (g_of[dg], q_of[dq % YZ])

    far_first = (4, 3, 5, 2, 6, 1, 7, 0)
    barrier = pltpu.get_barrier_semaphore()
    for dq in far_first:
        for dg in (1, -1, 0):
            if (dg, dq) != (0, 0):
                pl.semaphore_signal(barrier, inc=1, device_id=device(dg, dq), device_id_type=MESH)

    loads = [
        pltpu.make_async_copy(src, dst, load_sem.at[number])
        for number, (src, dst) in enumerate(
            (
                (tile_hbm, tile_in),
                (site_hbm, site_in),
                (stiff_hbm, stiff),
                (disp_hbm, disp),
                (solid_hbm, solid),
                (pop_hbm, start),
            )
        )
    ]
    for load in loads:
        load.start()

    sub = iota((8, LANES), 0)
    lane_group = iota((8, LANES), 1) // 8
    own_group = lane_group == sub

    vals[...] = jnp.zeros_like(vals)
    vals[6:7, :] = jnp.full((1, wide), -1.0, F32)
    upper = jnp.where(iota((LANES, LANES), 0) <= iota((LANES, LANES), 1), 1.0, 0.0).astype(BF16)
    for load in loads[0:4]:
        load.wait()
    tile = tile_in[...]
    vals[6:7, 0:marks] = ((tile & YZ) + ((tile - q) & (YZ - 1))).astype(F32)
    vals[0:1, 0:marks] = site_in[...].reshape(1, marks).astype(F32)
    stiffness = stiff[...].reshape(1, marks)
    vals[1:2, 0:marks] = stiffness
    vals[2:5, 0:marks] = -stiffness * disp[...]
    tile8 = jnp.broadcast_to(vals[6:7, :].astype(I32), (8, wide))
    sub_wide = iota((8, wide), 0)
    member = [jnp.where(tile8 == sub_wide + 8 * half, 1.0, 0.0) for half in range(2)]
    member = jnp.concatenate(member, axis=0)
    stacked = jnp.concatenate([member[:, b * LANES : (b + 1) * LANES] for b in range(blocks)], axis=0)
    counts = product(stacked.astype(BF16), upper, False)
    offset = jnp.full((TILES, 1), -1.0, F32)
    ranks = []
    for b in range(blocks):
        count = counts[b * TILES : (b + 1) * TILES, :]
        mine = member[:, b * LANES : (b + 1) * LANES]
        ranks.append(jnp.sum(mine * (count + offset), axis=0, keepdims=True))
        offset = offset + count[:, LANES - 1 : LANES]
    rank8 = jnp.broadcast_to(jnp.concatenate(ranks, axis=1).astype(I32), (8, wide))
    for top in range(0, LANES, 16):
        pair = [jnp.where(sub_wide + (top + more) == rank8, 1.0, 0.0) for more in (0, 8)]
        hot[top : top + 16, :] = jnp.concatenate(pair, axis=0).astype(BF16)
    over = jnp.where(sub_wide + LANES == rank8, 1.0, 0.0)
    over = jnp.concatenate([over, over], axis=0).astype(BF16)
    for top in range(LANES, 2 * LANES, 16):
        hot[top : top + 16, :] = over

    value = jnp.where(sub_wide < 5, vals[...], 0.0)
    binned = None
    for part in parts_of(value, BIN_PARTS):
        left = jnp.concatenate([jnp.where(tile8 == k, part, 0.0) for k in range(TILES)], axis=0)
        term = product(left.astype(BF16), hot[...], True)
        binned = term if binned is None else binned + term
    for k in range(TILES):
        main = binned[k * 8 : (k + 1) * 8, 0:LANES]
        more = binned[k * 8 : (k + 1) * 8, LANES : 2 * LANES]
        more = jnp.sum(jnp.where(own_group, more, 0.0), axis=0, keepdims=True)
        payload[k] = jnp.where(sub == 5, more, main)

    pl.semaphore_wait(barrier, 3 * YZ - 1)

    def whole(buffer, sem):
        pltpu.make_async_copy(buffer, buffer, sem).wait()

    for half in (1, 0):
        for dq in far_first:
            k = half * YZ + dq
            if k != 0:
                pltpu.make_async_remote_copy(
                    src_ref=payload.at[k, pl.ds(0, PUT_ROWS)],
                    dst_ref=recv.at[k, pl.ds(0, PUT_ROWS)],
                    send_sem=put_send,
                    recv_sem=put_recv.at[half],
                    device_id=device(half, dq),
                    device_id_type=MESH,
                ).start()

    rows32 = iota((32, LANES), 0)

    def place_group(k, block):
        site = block[0:1, :].astype(I32)
        place = ((site >> 12) << 7) + (site & 127)
        zhot[:, k * LANES : (k + 1) * LANES] = jnp.where(
            iota((2 * LANES, LANES), 0) == place, 1.0, 0.0
        ).astype(BF16)
        mask = rows32 == ((site >> 7) & 31)
        for number, part in enumerate(parts_of(block, STEP_PARTS)):
            for c in range(4):
                top = (number * 4 + c) * 32
                lhs[top : top + 32, k * LANES : (k + 1) * LANES] = jnp.where(
                    mask, part[1 + c : 2 + c, :], 0.0
                ).astype(BF16)

    tail = jnp.zeros((8, LANES), F32)
    for half in range(2):
        first = 1 if half == 0 else YZ
        whole(recv.at[pl.ds(first, (half + 1) * YZ - first), pl.ds(0, PUT_ROWS)], put_recv.at[half])
        for k in range(half * YZ, (half + 1) * YZ):
            block = payload[0] if k == 0 else recv[k]
            slots[k] = block
            more = jnp.where(own_group, jnp.broadcast_to(block[5:6, :], (8, LANES)), 0.0)
            tail = tail + jnp.where(lane_group == k, spread(more), 0.0)
            place_group(k, block)
    slots[TILES] = tail
    place_group(TILES, tail)
    result = product(lhs[...], zhot[...], True)
    total = result[0:128, :]
    for number in range(1, STEP_PARTS):
        total = total + result[number * 128 : (number + 1) * 128, :]
    field[...] = total
    for load in loads[4:]:
        load.wait()

    def pulled(step, index, a):
        cx, cy, cz = lattice_dirs[index]
        x_side = 0 if cx > 0 else 1
        y_side = 0 if cy > 0 else 1
        source = a - cx
        inside = 0 <= source < 8
        if inside:
            value = post[step % 2, index, source]
        else:
            value = halos[step, 5 * x_side + X_FACE[x_side].index(index)]
        if cy != 0:
            if inside:
                tile_of = 10 + 4 + 5 * y_side + Y_FACE[y_side].index(index)
                other = jnp.broadcast_to(halos[step, tile_of, source : source + 1, :], (8, LANES))
            else:
                other = halos[step, 10 + CORNER.index(index)]
            value = jnp.where(sub == (7 if cy > 0 else 0), other, value)
            value = pltpu.roll(value, cy % 8, 0)
        if cz != 0:
            value = pltpu.roll(value, cz % LANES, 1)
        return value

    def halo(step, src, first, count, dg, dq):
        pltpu.make_async_remote_copy(
            src_ref=edges.at[step, pl.ds(src, count)],
            dst_ref=halos.at[step, pl.ds(first, count)],
            send_sem=halo_send.at[step],
            recv_sem=halo_recv.at[step, 0 if first < 14 else 1],
            device_id=device(dg, dq),
            device_id_type=MESH,
        ).start()

    def send_x(step):
        for number, index in enumerate(CORNER):
            cx, cy, _ = lattice_dirs[index]
            side = 0 if cx > 0 else 1
            halo(step, 5 * side + X_FACE[side].index(index), 10 + number, 1, cx, cy)
        for side, dg in ((0, 1), (1, -1)):
            halo(step, 5 * side, 5 * side, 5, dg, 0)

    def send_y(step):
        for side, dq in ((0, 1), (1, -1)):
            halo(step, 10 + 5 * side, 14 + 5 * side, 5, 0, dq)

    def slice_step(step, a):
        if step == 0:
            popul = [start[index, a] for index in range(19)]
        else:
            popul = [pulled(step - 1, index, a) for index in range(19)]
        low = (a % 4) * 8
        high = (a // 4) * LANES
        stiff_sum, *forces = [field[c * 32 + low : c * 32 + low + 8, high : high + LANES] for c in range(4)]
        result, speed = collide(popul, forces, solid[a])
        for c in range(3):
            place = (slice(c * 32 + low, c * 32 + low + 8), slice(high, high + LANES))
            usum[place] = speed[c] if step == 0 else usum[place] + speed[c]
            if step < STEPS - 1:
                field[32 + c * 32 + low : 32 + c * 32 + low + 8, high : high + LANES] = (
                    forces[c] - stiff_sum * speed[c]
                )
        for index in range(19):
            post[step % 2, index, a] = result[index]
        for side, edge in ((0, 7), (1, 0)):
            if a == edge:
                for place, index in enumerate(X_FACE[side]):
                    edges[step, 5 * side + place] = result[index]
            for place, index in enumerate(Y_FACE[side]):
                edges[step, 10 + 5 * side + place, a : a + 1, :] = result[index][edge : edge + 1, :]

    for step in range(STEPS):
        if step == 0:
            slice_step(step, 0)
            slice_step(step, 7)
            send_x(step)
            for a in range(1, 7):
                slice_step(step, a)
            send_y(step)
        else:
            whole(halos.at[step - 1, pl.ds(14, 10)], halo_recv.at[step - 1, 1])
            for a in range(1, 7):
                slice_step(step, a)
            whole(halos.at[step - 1, pl.ds(0, 14)], halo_recv.at[step - 1, 0])
            slice_step(step, 0)
            slice_step(step, 7)
            send_x(step)
            send_y(step)

    left = jnp.concatenate([part.astype(BF16) for part in parts_of(usum[...], STEP_PARTS)], axis=0)
    sub4 = sub[0:4]
    moved = []
    for k in range(GROUPS):
        if k % 2 == 0:
            picked = product(left, zhot[:, k * LANES : min(k + 2, GROUPS) * LANES], False)
            total = picked[0:96, :]
            for number in range(1, STEP_PARTS):
                total = total + picked[number * 96 : (number + 1) * 96, :]
        mask = rows32 == ((slots[k][0:1, :].astype(I32) >> 7) & 31)
        lanes = slice((k % 2) * LANES, (k % 2 + 1) * LANES)
        block = jnp.zeros((8, LANES), F32)
        for c in range(3):
            speed = jnp.sum(
                jnp.where(mask, total[c * 32 : (c + 1) * 32, lanes], 0.0), axis=0, keepdims=True
            )
            block = jnp.where(sub == c, speed, block)
        moved.append(block)
    tail = moved[TILES]
    for half in (1, 0):
        for dq in far_first:
            k = half * YZ + dq
            more = spread(jnp.where(lane_group == k, tail, 0.0))
            more = jnp.sum(jnp.where(own_group, more, 0.0), axis=0, keepdims=True)
            block = jnp.where(sub == 3, more, moved[k])[0:4, :]
            if k == 0:
                ret[0] = block
            else:
                back[k] = block
                pltpu.make_async_remote_copy(
                    src_ref=back.at[k],
                    dst_ref=ret.at[k],
                    send_sem=ret_send,
                    recv_sem=ret_recv,
                    device_id=device(-half, -dq),
                    device_id_type=MESH,
                ).start()

    last = STEPS - 1
    whole(halos.at[last, pl.ds(14, 10)], halo_recv.at[last, 1])
    whole(halos.at[last, pl.ds(0, 14)], halo_recv.at[last, 0])
    for a in range(8):
        for index in range(19):
            out_ref[index, a] = pulled(last, index, a)
    for step in range(STEPS):
        whole(halos.at[step], halo_send.at[step])
    whole(recv.at[pl.ds(1, TILES - 1), pl.ds(0, PUT_ROWS)], put_send)

    whole(ret.at[pl.ds(1, TILES - 1)], ret_recv)
    own4 = own_group[0:4]
    lefts = []
    for k in range(TILES):
        block = ret[k]
        more = jnp.where(own4, jnp.broadcast_to(block[3:4, :], (4, LANES)), 0.0)
        lefts.append(jnp.concatenate([block, more], axis=1))
    left = jnp.concatenate(lefts, axis=0)
    left = jnp.concatenate([part.astype(BF16) for part in parts_of(left, BIN_PARTS)], axis=0)
    taken = product(left, hot[...], False)
    rows = 4 * TILES
    total = taken[0:rows, :]
    for number in range(1, BIN_PARTS):
        total = total + taken[number * rows : (number + 1) * rows, :]
    final = None
    tile8 = jnp.broadcast_to(vals[6:7, :].astype(I32), (8, wide)) - (sub_wide >> 2)
    for pair in range(YZ):
        term = jnp.where(tile8 == 2 * pair, total[pair * 8 : (pair + 1) * 8, :], 0.0)
        final = term if final is None else final + term
    final = final[0:4, :] + final[4:8, :]
    dout_ref[...] = disp[...] + final[0:3, 0:marks]
    whole(ret.at[pl.ds(1, TILES - 1)], ret_send)


def body(populations, solid, displacement, stiffness, marker_tile, marker_site):
    marks = displacement.shape[1]
    wide = -(-marks // LANES) * LANES
    vmem = pl.BlockSpec(memory_space=pltpu.VMEM)
    hbm = pl.BlockSpec(memory_space=pltpu.HBM)
    dma = pltpu.SemaphoreType.DMA
    return pl.pallas_call(
        kernel,
        out_shape=(
            jax.ShapeDtypeStruct(populations.shape, F32),
            jax.ShapeDtypeStruct(displacement.shape, F32),
        ),
        in_specs=[hbm] * 6,
        out_specs=(vmem, vmem),
        scratch_shapes=[
            pltpu.VMEM(populations.shape, F32),
            pltpu.VMEM(solid.shape, I32),
            pltpu.VMEM(displacement.shape, F32),
            pltpu.VMEM((marks,), F32),
            pltpu.VMEM((1, marks), I32),
            pltpu.VMEM((marks,), I32),
            pltpu.VMEM((8, wide), F32),
            pltpu.VMEM((2 * LANES, wide), BF16),
            pltpu.VMEM((TILES, 8, LANES), F32),
            pltpu.VMEM((TILES, 8, LANES), F32),
            pltpu.VMEM((2 * LANES, SLOTS), BF16),
            pltpu.VMEM((128 * STEP_PARTS, SLOTS), BF16),
            pltpu.VMEM((96, 2 * LANES), F32),
            pltpu.VMEM((128, 2 * LANES), F32),
            pltpu.VMEM((GROUPS, 8, LANES), F32),
            pltpu.VMEM((2,) + populations.shape, F32),
            pltpu.VMEM((STEPS, 20, 8, LANES), F32),
            pltpu.VMEM((STEPS, 24, 8, LANES), F32),
            pltpu.VMEM((TILES, 4, LANES), F32),
            pltpu.VMEM((TILES, 4, LANES), F32),
            dma((6,)),
            dma,
            dma((2,)),
            dma,
            dma,
            dma((STEPS,)),
            dma((STEPS, 2)),
        ],
        compiler_params=pltpu.CompilerParams(
            collective_id=0, has_side_effects=True, vmem_limit_bytes=16 * 1024 * 1024
        ),
        name="lattice_steps",
    )(
        *(
            pltpu.with_memory_space_constraint(value, pltpu.HBM)
            for value in (
                populations,
                solid,
                displacement,
                stiffness,
                marker_tile.reshape(1, -1),
                marker_site,
            )
        )
    )


def solution(mesh):
    in_specs = (
        P(None, "gx", "yz", None),
        P("gx", "yz", None),
        P(None, ("gx", "yz")),
        P(("gx", "yz")),
        P(("gx", "yz"), None),
        P(("gx", "yz")),
    )
    out_specs = (P(None, "gx", "yz", None), P(None, ("gx", "yz")))
    return jax.shard_map(body, mesh=mesh, in_specs=in_specs, out_specs=out_specs, check_vma=False)
```

```python
import functools

import jax
import jax.numpy as jnp
from jax import lax
from jax.experimental import pallas as pl
from jax.experimental.pallas import tpu as pltpu
from jax.sharding import PartitionSpec as P

MESH = pl.DeviceIdType.MESH
STEPS = 3
F32 = jnp.float32
BF16 = jnp.bfloat16
I32 = jnp.int32

lattice_dirs = [
    (0, 0, 0),
    (1, 0, 0),
    (-1, 0, 0),
    (0, 1, 0),
    (0, -1, 0),
    (0, 0, 1),
    (0, 0, -1),
    (1, 1, 0),
    (-1, -1, 0),
    (1, -1, 0),
    (-1, 1, 0),
    (1, 0, 1),
    (-1, 0, -1),
    (1, 0, -1),
    (-1, 0, 1),
    (0, 1, 1),
    (0, -1, -1),
    (0, 1, -1),
    (0, -1, 1),
]
lattice_weights = [1.0 / 3.0] + [1.0 / 18.0] * 6 + [1.0 / 36.0] * 12
relax_rate = 1.6
PUSH = 1.0 - 0.5 * relax_rate

X_FACE = [[1, 7, 9, 11, 13], [2, 8, 10, 12, 14]]
Y_FACE = [[3, 7, 10, 15, 17], [4, 8, 9, 16, 18]]
CORNER = [7, 8, 9, 10]

YZ = 8
TILES = 2 * YZ
LANES = 128
GROUPS = TILES + 1
SLOTS = GROUPS * LANES
BIN_PARTS = 2
PUT_ROWS = 6
STEP_PARTS = 2


def parts_of(value, count):
    parts = []
    rest = value
    for _ in range(count):
        part = rest.astype(BF16).astype(F32)
        parts.append(part)
        rest = rest - part
    return parts


def iota(shape, dim):
    return lax.broadcasted_iota(I32, shape, dim)


def spread(value):
    for shift in (8, 16, 32, 64):
        value = value + pltpu.roll(value, shift, 1)
    return value


def product(lhs, rhs, transposed):
    dims = (((1,), (1 if transposed else 0,)), ((), ()))
    return lax.dot_general(lhs, rhs, dims, preferred_element_type=F32)


def collide(popul, field, solid):
    density = popul[0]
    for index in range(1, 19):
        density = density + popul[index]
    moved = []
    for component in range(3):
        total = 0.5 * field[component]
        for index in range(1, 19, 2):
            offset = lattice_dirs[index][component]
            if offset > 0:
                total = total + (popul[index] - popul[index + 1])
            elif offset < 0:
                total = total - (popul[index] - popul[index + 1])
        moved.append(total)
    inverse = 1.0 / density
    speed = [total * inverse for total in moved]
    squared = speed[0] * speed[0] + speed[1] * speed[1] + speed[2] * speed[2]
    speed_field = speed[0] * field[0] + speed[1] * field[1] + speed[2] * field[2]
    dense = relax_rate * density
    base = dense - 1.5 * dense * squared - (3.0 * PUSH) * speed_field
    even = [(4.5 * relax_rate) * moved[c] + (9.0 * PUSH) * field[c] for c in range(3)]
    odd = [(3.0 * relax_rate) * moved[c] + (3.0 * PUSH) * field[c] for c in range(3)]
    wall = solid == 1
    keep = 1.0 - relax_rate
    result = [None] * 19
    result[0] = jnp.where(wall, popul[0], keep * popul[0] + lattice_weights[0] * base)

    def along(offsets, values):
        total = None
        for component in range(3):
            if offsets[component] != 0:
                term = values[component]
                if total is None:
                    total = term if offsets[component] > 0 else -term
                else:
                    total = total + term if offsets[component] > 0 else total - term
        return total

    for index in range(1, 19, 2):
        offsets = lattice_dirs[index]
        weight = lattice_weights[index]
        both = weight * (base + along(offsets, speed) * along(offsets, even))
        side = weight * along(offsets, odd)
        result[index] = jnp.where(wall, popul[index + 1], keep * popul[index] + (both + side))
        result[index + 1] = jnp.where(wall, popul[index], keep * popul[index + 1] + (both - side))
    return result, speed


def kernel(
    pop_hbm, solid_hbm, disp_hbm, stiff_hbm, tile_hbm, site_hbm,
    out_ref, dout_ref,
    start, solid, disp, stiff, tile_in, site_in, vals, hot, payload, recv, zhot, lhs, usum, field, slots,
    early, post, edges, halos, back, ret,
    load_sem, put_send, put_recv, ret_send, ret_recv, halo_send, halo_recv,
):
    marks = disp_hbm.shape[1]
    wide = vals.shape[1]
    blocks = wide // LANES
    n_gx = lax.axis_size("gx")
    g = lax.axis_index("gx")
    q = lax.axis_index("yz")
    g_of = {0: g, 1: lax.rem(g + 1, n_gx), -1: lax.rem(g + (n_gx - 1), n_gx)}
    q_of = [q if dq == 0 else (q + dq) & (YZ - 1) for dq in range(YZ)]

    def device(dg, dq):
        return (g_of[dg], q_of[dq % YZ])

    far_first = (4, 3, 5, 2, 6, 1, 7, 0)
    barrier = pltpu.get_barrier_semaphore()
    for dq in far_first:
        for dg in (-1, 0):
            if (dg, dq) != (0, 0):
                pl.semaphore_signal(barrier, inc=1, device_id=device(dg, dq), device_id_type=MESH)

    loads = [
        pltpu.make_async_copy(src, dst, load_sem.at[number])
        for number, (src, dst) in enumerate(
            (
                (tile_hbm, tile_in),
                (site_hbm, site_in),
                (stiff_hbm, stiff),
                (disp_hbm, disp),
                (solid_hbm, solid),
                (pop_hbm, start),
            )
        )
    ]
    for load in loads:
        load.start()

    sub = iota((8, LANES), 0)
    lane_group = iota((8, LANES), 1) // 8
    own_group = lane_group == sub

    vals[...] = jnp.zeros_like(vals)
    vals[6:7, :] = jnp.full((1, wide), -1.0, F32)
    upper = jnp.where(iota((LANES, LANES), 0) <= iota((LANES, LANES), 1), 1.0, 0.0).astype(BF16)
    for load in loads[0:4]:
        load.wait()
    tile = tile_in[...]
    vals[6:7, 0:marks] = ((tile & YZ) + ((tile - q) & (YZ - 1))).astype(F32)
    vals[0:1, 0:marks] = site_in[...].reshape(1, marks).astype(F32)
    stiffness = stiff[...].reshape(1, marks)
    vals[1:2, 0:marks] = stiffness
    vals[2:5, 0:marks] = -stiffness * disp[...]
    tile8 = jnp.broadcast_to(vals[6:7, :].astype(I32), (8, wide))
    sub_wide = iota((8, wide), 0)
    member = [jnp.where(tile8 == sub_wide + 8 * half, 1.0, 0.0) for half in range(2)]
    member = jnp.concatenate(member, axis=0)
    stacked = jnp.concatenate([member[:, b * LANES : (b + 1) * LANES] for b in range(blocks)], axis=0)
    counts = product(stacked.astype(BF16), upper, False)
    offset = jnp.full((TILES, 1), -1.0, F32)
    ranks = []
    for b in range(blocks):
        count = counts[b * TILES : (b + 1) * TILES, :]
        mine = member[:, b * LANES : (b + 1) * LANES]
        ranks.append(jnp.sum(mine * (count + offset), axis=0, keepdims=True))
        offset = offset + count[:, LANES - 1 : LANES]
    rank8 = jnp.broadcast_to(jnp.concatenate(ranks, axis=1).astype(I32), (8, wide))
    for top in range(0, LANES, 16):
        pair = [jnp.where(sub_wide + (top + more) == rank8, 1.0, 0.0) for more in (0, 8)]
        hot[top : top + 16, :] = jnp.concatenate(pair, axis=0).astype(BF16)
    over = jnp.where(sub_wide + LANES == rank8, 1.0, 0.0)
    over = jnp.concatenate([over, over], axis=0).astype(BF16)
    for top in range(LANES, 2 * LANES, 16):
        hot[top : top + 16, :] = over

    value = jnp.where(sub_wide < 5, vals[...], 0.0)
    binned = None
    for part in parts_of(value, BIN_PARTS):
        left = jnp.concatenate([jnp.where(tile8 == k, part, 0.0) for k in range(TILES)], axis=0)
        term = product(left.astype(BF16), hot[...], True)
        binned = term if binned is None else binned + term
    for k in range(TILES):
        main = binned[k * 8 : (k + 1) * 8, 0:LANES]
        more = binned[k * 8 : (k + 1) * 8, LANES : 2 * LANES]
        more = jnp.sum(jnp.where(own_group, more, 0.0), axis=0, keepdims=True)
        payload[k] = jnp.where(sub == 5, more, main)

    pl.semaphore_wait(barrier, 2 * YZ - 1)

    def whole(buffer, sem):
        pltpu.make_async_copy(buffer, buffer, sem).wait()

    for half in (1, 0):
        for dq in far_first:
            k = half * YZ + dq
            if k != 0:
                pltpu.make_async_remote_copy(
                    src_ref=payload.at[k, pl.ds(0, PUT_ROWS)],
                    dst_ref=recv.at[k, pl.ds(0, PUT_ROWS)],
                    send_sem=put_send,
                    recv_sem=put_recv.at[half],
                    device_id=device(half, dq),
                    device_id_type=MESH,
                ).start()

    rows32 = iota((32, LANES), 0)

    def place_group(k, block):
        site = block[0:1, :].astype(I32)
        place = ((site >> 12) << 7) + (site & 127)
        zhot[:, k * LANES : (k + 1) * LANES] = jnp.where(
            iota((2 * LANES, LANES), 0) == place, 1.0, 0.0
        ).astype(BF16)
        mask = rows32 == ((site >> 7) & 31)
        for number, part in enumerate(parts_of(block, STEP_PARTS)):
            for c in range(4):
                top = (number * 4 + c) * 32
                lhs[top : top + 32, k * LANES : (k + 1) * LANES] = jnp.where(
                    mask, part[1 + c : 2 + c, :], 0.0
                ).astype(BF16)

    tail = jnp.zeros((8, LANES), F32)
    for half in range(2):
        first = 1 if half == 0 else YZ
        whole(recv.at[pl.ds(first, (half + 1) * YZ - first), pl.ds(0, PUT_ROWS)], put_recv.at[half])
        for k in range(half * YZ, (half + 1) * YZ):
            block = payload[0] if k == 0 else recv[k]
            slots[k] = block
            more = jnp.where(own_group, jnp.broadcast_to(block[5:6, :], (8, LANES)), 0.0)
            tail = tail + jnp.where(lane_group == k, spread(more), 0.0)
            place_group(k, block)
        if half == 1:
            slots[TILES] = tail
            place_group(TILES, tail)
        lanes = slice(half * YZ * LANES, YZ * LANES if half == 0 else SLOTS)
        result = product(lhs[:, lanes], zhot[:, lanes], True)
        total = result[0:128, :]
        for number in range(1, STEP_PARTS):
            total = total + result[number * 128 : (number + 1) * 128, :]
        field[...] = total if half == 0 else field[...] + total
    for load in loads[4:]:
        load.wait()

    def pulled(step, index, a):
        cx, cy, cz = lattice_dirs[index]
        x_side = 0 if cx > 0 else 1
        y_side = 0 if cy > 0 else 1
        source = a - cx
        inside = 0 <= source < 8
        if inside:
            value = post[step % 2, index, source]
        else:
            value = halos[step, 5 * x_side + X_FACE[x_side].index(index)]
        if cy != 0:
            if inside:
                tile_of = 10 + 4 + 5 * y_side + Y_FACE[y_side].index(index)
                other = jnp.broadcast_to(halos[step, tile_of, source : source + 1, :], (8, LANES))
            else:
                other = halos[step, 10 + CORNER.index(index)]
            value = jnp.where(sub == (7 if cy > 0 else 0), other, value)
            value = pltpu.roll(value, cy % 8, 0)
        if cz != 0:
            value = pltpu.roll(value, cz % LANES, 1)
        return value

    def halo(step, src, first, count, dg, dq):
        pltpu.make_async_remote_copy(
            src_ref=edges.at[step, pl.ds(src, count)],
            dst_ref=halos.at[step, pl.ds(first, count)],
            send_sem=halo_send.at[step],
            recv_sem=halo_recv.at[step, 0 if first < 14 else 1],
            device_id=device(dg, dq),
            device_id_type=MESH,
        ).start()

    def send_x(step):
        for number, index in enumerate(CORNER):
            cx, cy, _ = lattice_dirs[index]
            side = 0 if cx > 0 else 1
            halo(step, 5 * side + X_FACE[side].index(index), 10 + number, 1, cx, cy)
        for side, dg in ((0, 1), (1, -1)):
            halo(step, 5 * side, 5 * side, 5, dg, 0)

    def send_y(step):
        for side, dq in ((0, 1), (1, -1)):
            halo(step, 10 + 5 * side, 14 + 5 * side, 5, 0, dq)

    def slice_step(step, a):
        if step == 0:
            popul = [start[index, a] for index in range(19)]
        else:
            popul = [pulled(step - 1, index, a) for index in range(19)]
        low = (a % 4) * 8
        high = (a // 4) * LANES
        stiff_sum, *forces = [field[c * 32 + low : c * 32 + low + 8, high : high + LANES] for c in range(4)]
        result, speed = collide(popul, forces, solid[a])
        for c in range(3):
            place = (slice(c * 32 + low, c * 32 + low + 8), slice(high, high + LANES))
            usum[place] = speed[c] if step == 0 else usum[place] + speed[c]
            if step < STEPS - 1:
                field[32 + c * 32 + low : 32 + c * 32 + low + 8, high : high + LANES] = (
                    forces[c] - stiff_sum * speed[c]
                )
        for index in range(19):
            post[step % 2, index, a] = result[index]
        for side, edge in ((0, 7), (1, 0)):
            if a == edge:
                for place, index in enumerate(X_FACE[side]):
                    edges[step, 5 * side + place] = result[index]
            for place, index in enumerate(Y_FACE[side]):
                edges[step, 10 + 5 * side + place, a : a + 1, :] = result[index][edge : edge + 1, :]

    def gather(lows):
        rows = [usum[c * 32 + low : c * 32 + low + 8, :] for c in range(3) for low in lows]
        count = 8 * len(rows)
        left = jnp.concatenate(rows, axis=0)
        left = jnp.concatenate([part.astype(BF16) for part in parts_of(left, STEP_PARTS)], axis=0)
        for k in range(GROUPS):
            if k % 2 == 0:
                picked = product(left, zhot[:, k * LANES : min(k + 2, GROUPS) * LANES], False)
                total = picked[0:count, :]
                for number in range(1, STEP_PARTS):
                    total = total + picked[number * count : (number + 1) * count, :]
            row = (slots[k][0:1, :].astype(I32) >> 7) & 31
            lanes = slice((k % 2) * LANES, (k % 2 + 1) * LANES)
            masks = [sub + low == row for low in lows]
            for c in range(3):
                speed = None
                for number, mask in enumerate(masks):
                    top = (c * len(lows) + number) * 8
                    term = jnp.where(mask, total[top : top + 8, lanes], 0.0)
                    speed = term if speed is None else speed + term
                yield k, c, speed

    for step in range(STEPS):
        if step == 0:
            slice_step(step, 0)
            slice_step(step, 7)
            send_x(step)
            for a in range(1, 7):
                slice_step(step, a)
            send_y(step)
        else:
            whole(halos.at[step - 1, pl.ds(14, 10)], halo_recv.at[step - 1, 1])
            for a in range(1, 7):
                slice_step(step, a)
            if step == STEPS - 1:
                for k, c, speed in gather((8, 16)):
                    early[k, c] = speed
            whole(halos.at[step - 1, pl.ds(0, 14)], halo_recv.at[step - 1, 0])
            slice_step(step, 0)
            slice_step(step, 7)
            send_x(step)
            send_y(step)

    moved = []
    for k, c, speed in gather((0, 24)):
        speed = jnp.sum(speed + early[k, c], axis=0, keepdims=True)
        if c == 0:
            moved.append(jnp.zeros((8, LANES), F32))
        moved[k] = jnp.where(sub == c, speed, moved[k])
    tail = moved[TILES]
    for half in (1, 0):
        for dq in far_first:
            k = half * YZ + dq
            more = spread(jnp.where(lane_group == k, tail, 0.0))
            more = jnp.sum(jnp.where(own_group, more, 0.0), axis=0, keepdims=True)
            block = jnp.where(sub == 3, more, moved[k])[0:4, :]
            if k == 0:
                ret[0] = block
            else:
                back[k] = block
                pltpu.make_async_remote_copy(
                    src_ref=back.at[k],
                    dst_ref=ret.at[k],
                    send_sem=ret_send,
                    recv_sem=ret_recv,
                    device_id=device(-half, -dq),
                    device_id_type=MESH,
                ).start()

    last = STEPS - 1
    whole(halos.at[last, pl.ds(14, 10)], halo_recv.at[last, 1])
    for a in range(1, 7):
        for index in range(19):
            out_ref[index, a] = pulled(last, index, a)
    whole(halos.at[last, pl.ds(0, 14)], halo_recv.at[last, 0])
    for a in (0, 7):
        for index in range(19):
            out_ref[index, a] = pulled(last, index, a)
    for step in range(STEPS):
        whole(halos.at[step], halo_send.at[step])
    whole(recv.at[pl.ds(1, TILES - 1), pl.ds(0, PUT_ROWS)], put_send)

    whole(ret.at[pl.ds(1, TILES - 1)], ret_recv)
    own4 = own_group[0:4]
    lefts = []
    for k in range(TILES):
        block = ret[k]
        more = jnp.where(own4, jnp.broadcast_to(block[3:4, :], (4, LANES)), 0.0)
        lefts.append(jnp.concatenate([block, more], axis=1))
    left = jnp.concatenate(lefts, axis=0)
    left = jnp.concatenate([part.astype(BF16) for part in parts_of(left, BIN_PARTS)], axis=0)
    taken = product(left, hot[...], False)
    rows = 4 * TILES
    total = taken[0:rows, :]
    for number in range(1, BIN_PARTS):
        total = total + taken[number * rows : (number + 1) * rows, :]
    final = None
    tile8 = jnp.broadcast_to(vals[6:7, :].astype(I32), (8, wide)) - (sub_wide >> 2)
    for pair in range(YZ):
        term = jnp.where(tile8 == 2 * pair, total[pair * 8 : (pair + 1) * 8, :], 0.0)
        final = term if final is None else final + term
    final = final[0:4, :] + final[4:8, :]
    dout_ref[...] = disp[...] + final[0:3, 0:marks]
    whole(ret.at[pl.ds(1, TILES - 1)], ret_send)


def flush(pop_ref, disp_ref, pop_hbm, disp_hbm, sems):
    copies = [pltpu.make_async_copy(disp_ref, disp_hbm, sems.at[0])]
    step = 4
    for number, first in enumerate(range(0, pop_ref.shape[0], step)):
        part = pl.ds(first, min(step, pop_ref.shape[0] - first))
        copies.append(pltpu.make_async_copy(pop_ref.at[part], pop_hbm.at[part], sems.at[number + 1]))
    for copy in copies:
        copy.start()
    for copy in copies:
        copy.wait()


def body(populations, solid, displacement, stiffness, marker_tile, marker_site):
    marks = displacement.shape[1]
    wide = -(-marks // LANES) * LANES
    vmem = pl.BlockSpec(memory_space=pltpu.VMEM)
    hbm = pl.BlockSpec(memory_space=pltpu.HBM)
    dma = pltpu.SemaphoreType.DMA
    final_pop, final_disp = pl.pallas_call(
        kernel,
        out_shape=(
            jax.ShapeDtypeStruct(populations.shape, F32),
            jax.ShapeDtypeStruct(displacement.shape, F32),
        ),
        in_specs=[hbm] * 6,
        out_specs=(vmem, vmem),
        scratch_shapes=[
            pltpu.VMEM(populations.shape, F32),
            pltpu.VMEM(solid.shape, I32),
            pltpu.VMEM(displacement.shape, F32),
            pltpu.VMEM((marks,), F32),
            pltpu.VMEM((1, marks), I32),
            pltpu.VMEM((marks,), I32),
            pltpu.VMEM((8, wide), F32),
            pltpu.VMEM((2 * LANES, wide), BF16),
            pltpu.VMEM((TILES, 8, LANES), F32),
            pltpu.VMEM((TILES, 8, LANES), F32),
            pltpu.VMEM((2 * LANES, SLOTS), BF16),
            pltpu.VMEM((128 * STEP_PARTS, SLOTS), BF16),
            pltpu.VMEM((96, 2 * LANES), F32),
            pltpu.VMEM((128, 2 * LANES), F32),
            pltpu.VMEM((GROUPS, 8, LANES), F32),
            pltpu.VMEM((GROUPS, 3, 8, LANES), F32),
            pltpu.VMEM((2,) + populations.shape, F32),
            pltpu.VMEM((STEPS, 20, 8, LANES), F32),
            pltpu.VMEM((STEPS, 24, 8, LANES), F32),
            pltpu.VMEM((TILES, 4, LANES), F32),
            pltpu.VMEM((TILES, 4, LANES), F32),
            dma((6,)),
            dma,
            dma((2,)),
            dma,
            dma,
            dma((STEPS,)),
            dma((STEPS, 2)),
        ],
        compiler_params=pltpu.CompilerParams(
            collective_id=0, has_side_effects=True, vmem_limit_bytes=16 * 1024 * 1024
        ),
        name="lattice_steps",
    )(
        *(
            pltpu.with_memory_space_constraint(value, pltpu.HBM)
            for value in (
                populations,
                solid,
                displacement,
                stiffness,
                marker_tile.reshape(1, -1),
                marker_site,
            )
        )
    )
    return pl.pallas_call(
        flush,
        out_shape=(
            jax.ShapeDtypeStruct(populations.shape, F32),
            jax.ShapeDtypeStruct(displacement.shape, F32),
        ),
        in_specs=[vmem, vmem],
        out_specs=(hbm, hbm),
        scratch_shapes=[dma((6,))],
        compiler_params=pltpu.CompilerParams(vmem_limit_bytes=16 * 1024 * 1024),
        name="write_out",
    )(final_pop, final_disp)


def solution(mesh):
    in_specs = (
        P(None, "gx", "yz", None),
        P("gx", "yz", None),
        P(None, ("gx", "yz")),
        P(("gx", "yz")),
        P(("gx", "yz"), None),
        P(("gx", "yz")),
    )
    out_specs = (P(None, "gx", "yz", None), P(None, ("gx", "yz")))
    return jax.shard_map(body, mesh=mesh, in_specs=in_specs, out_specs=out_specs, check_vma=False)
```

```python
import functools

import jax
import jax.numpy as jnp
from jax import lax
from jax.experimental import pallas as pl
from jax.experimental.pallas import tpu as pltpu
from jax.sharding import PartitionSpec as P

MESH = pl.DeviceIdType.MESH
F32 = jnp.float32
BF16 = jnp.bfloat16
I32 = jnp.int32

lattice_dirs = [
    (0, 0, 0),
    (1, 0, 0),
    (-1, 0, 0),
    (0, 1, 0),
    (0, -1, 0),
    (0, 0, 1),
    (0, 0, -1),
    (1, 1, 0),
    (-1, -1, 0),
    (1, -1, 0),
    (-1, 1, 0),
    (1, 0, 1),
    (-1, 0, -1),
    (1, 0, -1),
    (-1, 0, 1),
    (0, 1, 1),
    (0, -1, -1),
    (0, 1, -1),
    (0, -1, 1),
]
lattice_weights = [1.0 / 3.0] + [1.0 / 18.0] * 6 + [1.0 / 36.0] * 12
relax_rate = 1.6
PUSH = 1.0 - 0.5 * relax_rate

X_FACE = [[1, 7, 9, 11, 13], [2, 8, 10, 12, 14]]
Y_FACE = [[3, 7, 10, 15, 17], [4, 8, 9, 16, 18]]
CORNER = [7, 8, 9, 10]

YZ = 8
TILES = 2 * YZ
LANES = 128
GROUPS = TILES + 1
SLOTS = GROUPS * LANES
BIN_PARTS = 2
PUT_ROWS = 6
STEP_PARTS = 2


def parts_of(value, count):
    parts = []
    rest = value
    for _ in range(count):
        part = rest.astype(BF16).astype(F32)
        parts.append(part)
        rest = rest - part
    return parts


def iota(shape, dim):
    return lax.broadcasted_iota(I32, shape, dim)


def spread(value):
    for shift in (8, 16, 32, 64):
        value = value + pltpu.roll(value, shift, 1)
    return value


def product(lhs, rhs, transposed):
    dims = (((1,), (1 if transposed else 0,)), ((), ()))
    return lax.dot_general(lhs, rhs, dims, preferred_element_type=F32)


def collide(popul, field, solid):
    density = popul[0]
    for index in range(1, 19):
        density = density + popul[index]
    moved = []
    for component in range(3):
        total = 0.5 * field[component]
        for index in range(1, 19, 2):
            offset = lattice_dirs[index][component]
            if offset > 0:
                total = total + (popul[index] - popul[index + 1])
            elif offset < 0:
                total = total - (popul[index] - popul[index + 1])
        moved.append(total)
    inverse = 1.0 / density
    speed = [total * inverse for total in moved]
    squared = speed[0] * speed[0] + speed[1] * speed[1] + speed[2] * speed[2]
    speed_field = speed[0] * field[0] + speed[1] * field[1] + speed[2] * field[2]
    dense = relax_rate * density
    base = dense - 1.5 * dense * squared - (3.0 * PUSH) * speed_field
    even = [(4.5 * relax_rate) * moved[c] + (9.0 * PUSH) * field[c] for c in range(3)]
    odd = [(3.0 * relax_rate) * moved[c] + (3.0 * PUSH) * field[c] for c in range(3)]
    wall = solid == 1
    keep = 1.0 - relax_rate
    result = [None] * 19
    result[0] = jnp.where(wall, popul[0], keep * popul[0] + lattice_weights[0] * base)

    def along(offsets, values):
        total = None
        for component in range(3):
            if offsets[component] != 0:
                term = values[component]
                if total is None:
                    total = term if offsets[component] > 0 else -term
                else:
                    total = total + term if offsets[component] > 0 else total - term
        return total

    for index in range(1, 19, 2):
        offsets = lattice_dirs[index]
        weight = lattice_weights[index]
        both = weight * (base + along(offsets, speed) * along(offsets, even))
        side = weight * along(offsets, odd)
        result[index] = jnp.where(wall, popul[index + 1], keep * popul[index] + (both + side))
        result[index + 1] = jnp.where(wall, popul[index], keep * popul[index + 1] + (both - side))
    return result, speed


def kernel(
    pop_hbm, solid_hbm, disp_hbm, stiff_hbm, tile_hbm, site_hbm,
    out_ref, dout_ref,
    start, solid, disp, stiff, tile_in, site_in, vals, hot, payload, recv, zhot, lhs, usum, field, slots,
    main, skirt, main_next, skirt_next, post, edges, halos, back, ret,
    load_sem, put_send, put_recv, ret_send, ret_recv, halo_send, halo_recv,
):
    marks = disp_hbm.shape[1]
    wide = vals.shape[1]
    blocks = wide // LANES
    n_gx = lax.axis_size("gx")
    g = lax.axis_index("gx")
    q = lax.axis_index("yz")
    g_of = {0: g, 1: lax.rem(g + 1, n_gx), -1: lax.rem(g + (n_gx - 1), n_gx)}
    q_of = [q if dq == 0 else (q + dq) & (YZ - 1) for dq in range(YZ)]

    def device(dg, dq):
        return (g_of[dg], q_of[dq % YZ])

    far_first = (4, 3, 5, 2, 6, 1, 7, 0)
    barrier = pltpu.get_barrier_semaphore()
    for dq in far_first:
        for dg in (-1, 0):
            if (dg, dq) != (0, 0):
                pl.semaphore_signal(barrier, inc=1, device_id=device(dg, dq), device_id_type=MESH)

    loads = [
        pltpu.make_async_copy(src, dst, load_sem.at[number])
        for number, (src, dst) in enumerate(
            (
                (tile_hbm, tile_in),
                (site_hbm, site_in),
                (stiff_hbm, stiff),
                (disp_hbm, disp),
                (solid_hbm, solid),
                (pop_hbm, start),
            )
        )
    ]
    for load in loads:
        load.start()

    sub = iota((8, LANES), 0)
    lane_group = iota((8, LANES), 1) // 8
    own_group = lane_group == sub

    vals[...] = jnp.zeros_like(vals)
    vals[6:7, :] = jnp.full((1, wide), -1.0, F32)
    upper = jnp.where(iota((LANES, LANES), 0) <= iota((LANES, LANES), 1), 1.0, 0.0).astype(BF16)
    for load in loads[0:4]:
        load.wait()
    tile = tile_in[...]
    vals[6:7, 0:marks] = ((tile & YZ) + ((tile - q) & (YZ - 1))).astype(F32)
    vals[0:1, 0:marks] = site_in[...].reshape(1, marks).astype(F32)
    stiffness = stiff[...].reshape(1, marks)
    vals[1:2, 0:marks] = stiffness
    vals[2:5, 0:marks] = -stiffness * disp[...]
    tile8 = jnp.broadcast_to(vals[6:7, :].astype(I32), (8, wide))
    sub_wide = iota((8, wide), 0)
    member = [jnp.where(tile8 == sub_wide + 8 * half, 1.0, 0.0) for half in range(2)]
    member = jnp.concatenate(member, axis=0)
    stacked = jnp.concatenate([member[:, b * LANES : (b + 1) * LANES] for b in range(blocks)], axis=0)
    counts = product(stacked.astype(BF16), upper, False)
    offset = jnp.full((TILES, 1), -1.0, F32)
    ranks = []
    for b in range(blocks):
        count = counts[b * TILES : (b + 1) * TILES, :]
        mine = member[:, b * LANES : (b + 1) * LANES]
        ranks.append(jnp.sum(mine * (count + offset), axis=0, keepdims=True))
        offset = offset + count[:, LANES - 1 : LANES]
    rank8 = jnp.broadcast_to(jnp.concatenate(ranks, axis=1).astype(I32), (8, wide))
    for top in range(0, LANES, 16):
        pair = [jnp.where(sub_wide + (top + more) == rank8, 1.0, 0.0) for more in (0, 8)]
        hot[top : top + 16, :] = jnp.concatenate(pair, axis=0).astype(BF16)
    over = jnp.where(sub_wide + LANES == rank8, 1.0, 0.0)
    over = jnp.concatenate([over, over], axis=0).astype(BF16)
    for top in range(LANES, 2 * LANES, 16):
        hot[top : top + 16, :] = over

    value = jnp.where(sub_wide < 5, vals[...], 0.0)
    binned = None
    for part in parts_of(value, BIN_PARTS):
        left = jnp.concatenate([jnp.where(tile8 == k, part, 0.0) for k in range(TILES)], axis=0)
        term = product(left.astype(BF16), hot[...], True)
        binned = term if binned is None else binned + term
    for k in range(TILES):
        low_ranks = binned[k * 8 : (k + 1) * 8, 0:LANES]
        more = binned[k * 8 : (k + 1) * 8, LANES : 2 * LANES]
        more = jnp.sum(jnp.where(own_group, more, 0.0), axis=0, keepdims=True)
        payload[k] = jnp.where(sub == 5, more, low_ranks)

    pl.semaphore_wait(barrier, 2 * YZ - 1)

    def whole(buffer, sem):
        pltpu.make_async_copy(buffer, buffer, sem).wait()

    for half in (1, 0):
        for dq in far_first:
            k = half * YZ + dq
            if k != 0:
                pltpu.make_async_remote_copy(
                    src_ref=payload.at[k, pl.ds(0, PUT_ROWS)],
                    dst_ref=recv.at[k, pl.ds(0, PUT_ROWS)],
                    send_sem=put_send,
                    recv_sem=put_recv.at[half],
                    device_id=device(half, dq),
                    device_id_type=MESH,
                ).start()

    rows32 = iota((32, LANES), 0)

    def place_group(k, block):
        site = block[0:1, :].astype(I32)
        place = ((site >> 12) << 7) + (site & 127)
        zhot[:, k * LANES : (k + 1) * LANES] = jnp.where(
            iota((2 * LANES, LANES), 0) == place, 1.0, 0.0
        ).astype(BF16)
        mask = rows32 == ((site >> 7) & 31)
        for number, part in enumerate(parts_of(block, STEP_PARTS)):
            for c in range(4):
                top = (number * 4 + c) * 32
                lhs[top : top + 32, k * LANES : (k + 1) * LANES] = jnp.where(
                    mask, part[1 + c : 2 + c, :], 0.0
                ).astype(BF16)

    tail = jnp.zeros((8, LANES), F32)
    for half in range(2):
        first = 1 if half == 0 else YZ
        whole(recv.at[pl.ds(first, (half + 1) * YZ - first), pl.ds(0, PUT_ROWS)], put_recv.at[half])
        for k in range(half * YZ, (half + 1) * YZ):
            block = payload[0] if k == 0 else recv[k]
            slots[k] = block
            more = jnp.where(own_group, jnp.broadcast_to(block[5:6, :], (8, LANES)), 0.0)
            tail = tail + jnp.where(lane_group == k, spread(more), 0.0)
            place_group(k, block)
        if half == 1:
            slots[TILES] = tail
            place_group(TILES, tail)
        lanes = slice(half * YZ * LANES, YZ * LANES if half == 0 else SLOTS)
        result = product(lhs[:, lanes], zhot[:, lanes], True)
        total = result[0:128, :]
        for number in range(1, STEP_PARTS):
            total = total + result[number * 128 : (number + 1) * 128, :]
        field[...] = total if half == 0 else field[...] + total
    for load in loads[4:]:
        load.wait()

    def streamed(index, main, skirt):
        _, cy, cz = lattice_dirs[index]
        value = main
        if cy != 0:
            value = jnp.where(sub == (7 if cy > 0 else 0), skirt, main)
            value = pltpu.roll(value, cy % 8, 0)
        if cz != 0:
            value = pltpu.roll(value, cz % LANES, 1)
        return value

    def remote(src, dst, send, recv_of, dg, dq):
        pltpu.make_async_remote_copy(
            src_ref=src,
            dst_ref=dst,
            send_sem=send,
            recv_sem=recv_of,
            device_id=device(dg, dq),
            device_id_type=MESH,
        ).start()

    def margin(channels, ax, ay, dg, dq, which):
        first, count = channels
        part = pl.ds(first, count)
        a_src, a_dst = {0: (2, 2), 1: (10 - ax, 2 - ax), -1: (2, 10)}[dg]
        slices = ax if dg != 0 else 8
        b_src = {0: 0, 1: 8 - ay, -1: 0}[dq]
        rows = pl.ds(b_src, ay if dq != 0 else 8)
        into = main if dq == 0 else skirt
        remote(
            main.at[part, pl.ds(a_src, slices), rows],
            into.at[part, pl.ds(a_dst, slices), rows],
            halo_send.at[0, which],
            halo_recv.at[0, which],
            dg,
            dq,
        )

    def margin_x():
        for index in CORNER:
            dg, dq, _ = lattice_dirs[index]
            margin((index, 1), 2, 2, dg, dq, 0)
            margin((0, 7), 2, 2, dg, dq, 0)
            margin((11, 4), 2, 1, dg, dq, 0)
            margin((15, 4), 1, 2, dg, dq, 0)
            margin((19, 4), 1, 1, dg, dq, 0)
        for side, dg in ((0, 1), (1, -1)):
            for index in X_FACE[side]:
                margin((index, 1), 2, 0, dg, 0, 0)
            for channels in ((0, 1), (3, 4), (15, 8)):
                margin(channels, 1, 0, dg, 0, 0)

    def margin_y():
        for side, dq in ((0, 1), (1, -1)):
            for index in Y_FACE[side]:
                margin((index, 1), 0, 2, 0, dq, 1)
            for channels in ((0, 3), (5, 2), (11, 4), (19, 4)):
                margin(channels, 0, 1, 0, dq, 1)

    def span(a):
        low = (a % 4) * 8
        high = (a // 4) * LANES
        return [(slice(c * 32 + low, c * 32 + low + 8), slice(high, high + LANES)) for c in range(4)]

    def first_step(a):
        spans = span(a)
        stiff_sum, *forces = [field[place] for place in spans]
        result, speed = collide([start[index, a] for index in range(19)], forces, solid[a])
        for index in range(19):
            main[index, a + 2] = result[index]
        for c in range(3):
            usum[spans[c]] = speed[c]
            main[19 + c, a + 2] = forces[c] - stiff_sum * speed[c]
        main[22, a + 2] = solid[a].astype(F32)

    def second_step(a, outside):
        own, other = (skirt, main) if outside else (main, skirt)
        popul = []
        for index in range(19):
            source = a - lattice_dirs[index][0] + 2
            popul.append(streamed(index, own[index, source], other[index, source]))
        forces = [own[19 + c, a + 2] for c in range(3)]
        result, speed = collide(popul, forces, own[22, a + 2])
        for index in range(19):
            (skirt_next if outside else main_next)[index, a + 1] = result[index]
        if not outside and 0 <= a < 8:
            spans = span(a)
            stiff_sum = field[spans[0]]
            for c in range(3):
                usum[spans[c]] = usum[spans[c]] + speed[c]
                field[spans[c + 1]] = forces[c] - stiff_sum * speed[c]

    def third_step(a):
        popul = []
        for index in range(19):
            source = a - lattice_dirs[index][0] + 1
            popul.append(streamed(index, main_next[index, source], skirt_next[index, source]))
        spans = span(a)
        result, speed = collide(popul, [field[place] for place in spans[1:]], solid[a])
        for c in range(3):
            usum[spans[c]] = usum[spans[c]] + speed[c]
        for index in range(19):
            post[index, a] = result[index]
        for side, edge in ((0, 7), (1, 0)):
            if a == edge:
                for place, index in enumerate(X_FACE[side]):
                    edges[5 * side + place] = result[index]
            for place, index in enumerate(Y_FACE[side]):
                edges[10 + 5 * side + place, a : a + 1, :] = result[index][edge : edge + 1, :]

    def halo(src, first, count, dg, dq):
        which = 0 if first < 14 else 1
        remote(
            edges.at[pl.ds(src, count)],
            halos.at[pl.ds(first, count)],
            halo_send.at[1, which],
            halo_recv.at[1, which],
            dg,
            dq,
        )

    def pulled(index, a):
        cx, cy, _ = lattice_dirs[index]
        x_side = 0 if cx > 0 else 1
        y_side = 0 if cy > 0 else 1
        source = a - cx
        inside = 0 <= source < 8
        value = post[index, source] if inside else halos[5 * x_side + X_FACE[x_side].index(index)]
        other = value
        if cy != 0:
            if inside:
                tile_of = 14 + 5 * y_side + Y_FACE[y_side].index(index)
                other = jnp.broadcast_to(halos[tile_of, source : source + 1, :], (8, LANES))
            else:
                other = halos[10 + CORNER.index(index)]
        return streamed(index, value, other)

    def gather():
        left = jnp.concatenate([part.astype(BF16) for part in parts_of(usum[...], STEP_PARTS)], axis=0)
        for k in range(GROUPS):
            if k % 2 == 0:
                picked = product(left, zhot[:, k * LANES : min(k + 2, GROUPS) * LANES], False)
                total = picked[0:96, :]
                for number in range(1, STEP_PARTS):
                    total = total + picked[number * 96 : (number + 1) * 96, :]
            mask = rows32 == ((slots[k][0:1, :].astype(I32) >> 7) & 31)
            lanes = slice((k % 2) * LANES, (k % 2 + 1) * LANES)
            for c in range(3):
                speed = jnp.where(mask, total[c * 32 : (c + 1) * 32, lanes], 0.0)
                yield k, c, jnp.sum(speed, axis=0, keepdims=True)

    for a in (0, 1, 6, 7):
        first_step(a)
    margin_x()
    for a in range(2, 6):
        first_step(a)
    margin_y()
    whole(main.at[:, pl.ds(0, 2)], halo_recv.at[0, 1])
    for a in range(1, 7):
        second_step(a, False)
        second_step(a, True)
    for a in range(2, 6):
        third_step(a)
    whole(main.at[pl.ds(0, 6)], halo_recv.at[0, 0])
    for a in (-1, 0, 7, 8):
        second_step(a, False)
        second_step(a, True)
    third_step(0)
    third_step(7)
    for number, index in enumerate(CORNER):
        cx, cy, _ = lattice_dirs[index]
        side = 0 if cx > 0 else 1
        halo(5 * side + X_FACE[side].index(index), 10 + number, 1, cx, cy)
    for side, dg in ((0, 1), (1, -1)):
        halo(5 * side, 5 * side, 5, dg, 0)
    third_step(1)
    third_step(6)
    for side, dq in ((0, 1), (1, -1)):
        halo(10 + 5 * side, 14 + 5 * side, 5, 0, dq)

    moved = []
    for k, c, speed in gather():
        if c == 0:
            moved.append(jnp.zeros((8, LANES), F32))
        moved[k] = jnp.where(sub == c, speed, moved[k])
    tail = moved[TILES]
    for half in (1, 0):
        for dq in far_first:
            k = half * YZ + dq
            more = spread(jnp.where(lane_group == k, tail, 0.0))
            more = jnp.sum(jnp.where(own_group, more, 0.0), axis=0, keepdims=True)
            block = jnp.where(sub == 3, more, moved[k])[0:4, :]
            if k == 0:
                ret[0] = block
            else:
                back[k] = block
                pltpu.make_async_remote_copy(
                    src_ref=back.at[k],
                    dst_ref=ret.at[k],
                    send_sem=ret_send,
                    recv_sem=ret_recv,
                    device_id=device(-half, -dq),
                    device_id_type=MESH,
                ).start()

    whole(halos.at[pl.ds(14, 10)], halo_recv.at[1, 1])
    for a in range(1, 7):
        for index in range(19):
            out_ref[index, a] = pulled(index, a)
    whole(halos.at[pl.ds(0, 14)], halo_recv.at[1, 0])
    for a in (0, 7):
        for index in range(19):
            out_ref[index, a] = pulled(index, a)
    whole(main.at[pl.ds(0, 6)], halo_send.at[0, 0])
    whole(main.at[:, pl.ds(0, 2)], halo_send.at[0, 1])
    whole(halos.at[pl.ds(0, 14)], halo_send.at[1, 0])
    whole(halos.at[pl.ds(14, 10)], halo_send.at[1, 1])
    whole(recv.at[pl.ds(1, TILES - 1), pl.ds(0, PUT_ROWS)], put_send)

    whole(ret.at[pl.ds(1, TILES - 1)], ret_recv)
    own4 = own_group[0:4]
    lefts = []
    for k in range(TILES):
        block = ret[k]
        more = jnp.where(own4, jnp.broadcast_to(block[3:4, :], (4, LANES)), 0.0)
        lefts.append(jnp.concatenate([block, more], axis=1))
    left = jnp.concatenate(lefts, axis=0)
    left = jnp.concatenate([part.astype(BF16) for part in parts_of(left, BIN_PARTS)], axis=0)
    taken = product(left, hot[...], False)
    rows = 4 * TILES
    total = taken[0:rows, :]
    for number in range(1, BIN_PARTS):
        total = total + taken[number * rows : (number + 1) * rows, :]
    final = None
    tile8 = jnp.broadcast_to(vals[6:7, :].astype(I32), (8, wide)) - (sub_wide >> 2)
    for pair in range(YZ):
        term = jnp.where(tile8 == 2 * pair, total[pair * 8 : (pair + 1) * 8, :], 0.0)
        final = term if final is None else final + term
    final = final[0:4, :] + final[4:8, :]
    dout_ref[...] = disp[...] + final[0:3, 0:marks]
    whole(ret.at[pl.ds(1, TILES - 1)], ret_send)


def flush(pop_ref, disp_ref, pop_hbm, disp_hbm, sems):
    copies = [pltpu.make_async_copy(disp_ref, disp_hbm, sems.at[0])]
    step = 4
    for number, first in enumerate(range(0, pop_ref.shape[0], step)):
        part = pl.ds(first, min(step, pop_ref.shape[0] - first))
        copies.append(pltpu.make_async_copy(pop_ref.at[part], pop_hbm.at[part], sems.at[number + 1]))
    for copy in copies:
        copy.start()
    for copy in copies:
        copy.wait()


def body(populations, solid, displacement, stiffness, marker_tile, marker_site):
    marks = displacement.shape[1]
    wide = -(-marks // LANES) * LANES
    vmem = pl.BlockSpec(memory_space=pltpu.VMEM)
    hbm = pl.BlockSpec(memory_space=pltpu.HBM)
    dma = pltpu.SemaphoreType.DMA
    final_pop, final_disp = pl.pallas_call(
        kernel,
        out_shape=(
            jax.ShapeDtypeStruct(populations.shape, F32),
            jax.ShapeDtypeStruct(displacement.shape, F32),
        ),
        in_specs=[hbm] * 6,
        out_specs=(vmem, vmem),
        scratch_shapes=[
            pltpu.VMEM(populations.shape, F32),
            pltpu.VMEM(solid.shape, I32),
            pltpu.VMEM(displacement.shape, F32),
            pltpu.VMEM((marks,), F32),
            pltpu.VMEM((1, marks), I32),
            pltpu.VMEM((marks,), I32),
            pltpu.VMEM((8, wide), F32),
            pltpu.VMEM((2 * LANES, wide), BF16),
            pltpu.VMEM((TILES, 8, LANES), F32),
            pltpu.VMEM((TILES, 8, LANES), F32),
            pltpu.VMEM((2 * LANES, SLOTS), BF16),
            pltpu.VMEM((128 * STEP_PARTS, SLOTS), BF16),
            pltpu.VMEM((96, 2 * LANES), F32),
            pltpu.VMEM((128, 2 * LANES), F32),
            pltpu.VMEM((GROUPS, 8, LANES), F32),
            pltpu.VMEM((23, 12, 8, LANES), F32),
            pltpu.VMEM((23, 12, 8, LANES), F32),
            pltpu.VMEM((19, 10, 8, LANES), F32),
            pltpu.VMEM((19, 10, 8, LANES), F32),
            pltpu.VMEM(populations.shape, F32),
            pltpu.VMEM((20, 8, LANES), F32),
            pltpu.VMEM((24, 8, LANES), F32),
            pltpu.VMEM((TILES, 4, LANES), F32),
            pltpu.VMEM((TILES, 4, LANES), F32),
            dma((6,)),
            dma,
            dma((2,)),
            dma,
            dma,
            dma((2, 2)),
            dma((2, 2)),
        ],
        compiler_params=pltpu.CompilerParams(
            collective_id=0, has_side_effects=True, vmem_limit_bytes=16 * 1024 * 1024
        ),
        name="lattice_steps",
    )(
        *(
            pltpu.with_memory_space_constraint(value, pltpu.HBM)
            for value in (
                populations,
                solid,
                displacement,
                stiffness,
                marker_tile.reshape(1, -1),
                marker_site,
            )
        )
    )
    return pl.pallas_call(
        flush,
        out_shape=(
            jax.ShapeDtypeStruct(populations.shape, F32),
            jax.ShapeDtypeStruct(displacement.shape, F32),
        ),
        in_specs=[vmem, vmem],
        out_specs=(hbm, hbm),
        scratch_shapes=[dma((6,))],
        compiler_params=pltpu.CompilerParams(vmem_limit_bytes=16 * 1024 * 1024),
        name="write_out",
    )(final_pop, final_disp)


def solution(mesh):
    in_specs = (
        P(None, "gx", "yz", None),
        P("gx", "yz", None),
        P(None, ("gx", "yz")),
        P(("gx", "yz")),
        P(("gx", "yz"), None),
        P(("gx", "yz")),
    )
    out_specs = (P(None, "gx", "yz", None), P(None, ("gx", "yz")))
    return jax.shard_map(body, mesh=mesh, in_specs=in_specs, out_specs=out_specs, check_vma=False)
```

```python
import functools

import jax
import jax.numpy as jnp
from jax import lax
from jax.experimental import pallas as pl
from jax.experimental.pallas import tpu as pltpu
from jax.sharding import PartitionSpec as P

MESH = pl.DeviceIdType.MESH
F32 = jnp.float32
BF16 = jnp.bfloat16
I32 = jnp.int32

lattice_dirs = [
    (0, 0, 0),
    (1, 0, 0),
    (-1, 0, 0),
    (0, 1, 0),
    (0, -1, 0),
    (0, 0, 1),
    (0, 0, -1),
    (1, 1, 0),
    (-1, -1, 0),
    (1, -1, 0),
    (-1, 1, 0),
    (1, 0, 1),
    (-1, 0, -1),
    (1, 0, -1),
    (-1, 0, 1),
    (0, 1, 1),
    (0, -1, -1),
    (0, 1, -1),
    (0, -1, 1),
]
lattice_weights = [1.0 / 3.0] + [1.0 / 18.0] * 6 + [1.0 / 36.0] * 12
relax_rate = 1.6
PUSH = 1.0 - 0.5 * relax_rate

X_FACE = [[1, 7, 9, 11, 13], [2, 8, 10, 12, 14]]
Y_FACE = [[3, 7, 10, 15, 17], [4, 8, 9, 16, 18]]
CORNER = [7, 8, 9, 10]

CHANNELS = [7, 1, 11, 13, 9, 3, 15, 17, 0, 5, 6, 19, 20, 21, 22, 4, 16, 18, 10, 2, 12, 14, 8]
SPOT = {channel: place for place, channel in enumerate(CHANNELS)}
RUNS = {
    (1, 1): (0, 1), (1, 0): (1, 3), (1, -1): (4, 1),
    (0, 1): (5, 3), (0, 0): (8, 7), (0, -1): (15, 3),
    (-1, 1): (18, 1), (-1, 0): (19, 3), (-1, -1): (22, 1),
}

YZ = 8
TILES = 2 * YZ
LANES = 128
GROUPS = TILES + 1
SLOTS = GROUPS * LANES
BIN_PARTS = 2
PUT_ROWS = 6
STEP_PARTS = 2


def parts_of(value, count):
    parts = []
    rest = value
    for _ in range(count):
        part = rest.astype(BF16).astype(F32)
        parts.append(part)
        rest = rest - part
    return parts


def iota(shape, dim):
    return lax.broadcasted_iota(I32, shape, dim)


def spread(value):
    for shift in (8, 16, 32, 64):
        value = value + pltpu.roll(value, shift, 1)
    return value


def product(lhs, rhs, transposed):
    dims = (((1,), (1 if transposed else 0,)), ((), ()))
    return lax.dot_general(lhs, rhs, dims, preferred_element_type=F32)


def collide(popul, field, solid):
    density = popul[0]
    for index in range(1, 19):
        density = density + popul[index]
    moved = []
    for component in range(3):
        total = 0.5 * field[component]
        for index in range(1, 19, 2):
            offset = lattice_dirs[index][component]
            if offset > 0:
                total = total + (popul[index] - popul[index + 1])
            elif offset < 0:
                total = total - (popul[index] - popul[index + 1])
        moved.append(total)
    inverse = 1.0 / density
    speed = [total * inverse for total in moved]
    squared = speed[0] * speed[0] + speed[1] * speed[1] + speed[2] * speed[2]
    speed_field = speed[0] * field[0] + speed[1] * field[1] + speed[2] * field[2]
    dense = relax_rate * density
    base = dense - 1.5 * dense * squared - (3.0 * PUSH) * speed_field
    even = [(4.5 * relax_rate) * moved[c] + (9.0 * PUSH) * field[c] for c in range(3)]
    odd = [(3.0 * relax_rate) * moved[c] + (3.0 * PUSH) * field[c] for c in range(3)]
    wall = solid == 1
    keep = 1.0 - relax_rate
    result = [None] * 19
    result[0] = jnp.where(wall, popul[0], keep * popul[0] + lattice_weights[0] * base)

    def along(offsets, values):
        total = None
        for component in range(3):
            if offsets[component] != 0:
                term = values[component]
                if total is None:
                    total = term if offsets[component] > 0 else -term
                else:
                    total = total + term if offsets[component] > 0 else total - term
        return total

    for index in range(1, 19, 2):
        offsets = lattice_dirs[index]
        weight = lattice_weights[index]
        both = weight * (base + along(offsets, speed) * along(offsets, even))
        side = weight * along(offsets, odd)
        result[index] = jnp.where(wall, popul[index + 1], keep * popul[index] + (both + side))
        result[index + 1] = jnp.where(wall, popul[index], keep * popul[index + 1] + (both - side))
    return result, speed


def kernel(
    pop_hbm, solid_hbm, disp_hbm, stiff_hbm, tile_hbm, site_hbm,
    out_ref, dout_ref,
    start, solid, disp, stiff, tile_in, site_in, vals, hot, payload, recv, zhot, lhs, usum, field, slots,
    main, skirt, main_next, skirt_next, post, edges, halos, back, ret,
    load_sem, put_send, put_recv, ret_send, ret_recv, halo_send, halo_recv,
):
    marks = disp_hbm.shape[1]
    wide = vals.shape[1]
    blocks = wide // LANES
    n_gx = lax.axis_size("gx")
    g = lax.axis_index("gx")
    q = lax.axis_index("yz")
    g_of = {0: g, 1: lax.rem(g + 1, n_gx), -1: lax.rem(g + (n_gx - 1), n_gx)}
    q_of = [q if dq == 0 else (q + dq) & (YZ - 1) for dq in range(YZ)]

    def device(dg, dq):
        return (g_of[dg], q_of[dq % YZ])

    far_first = (4, 3, 5, 2, 6, 1, 7, 0)
    barrier = pltpu.get_barrier_semaphore()
    for dq in far_first:
        for dg in (-1, 0):
            if (dg, dq) != (0, 0):
                pl.semaphore_signal(barrier, inc=1, device_id=device(dg, dq), device_id_type=MESH)

    loads = [
        pltpu.make_async_copy(src, dst, load_sem.at[number])
        for number, (src, dst) in enumerate(
            (
                (tile_hbm, tile_in),
                (site_hbm, site_in),
                (stiff_hbm, stiff),
                (disp_hbm, disp),
                (solid_hbm, solid),
                (pop_hbm, start),
            )
        )
    ]
    for load in loads:
        load.start()

    sub = iota((8, LANES), 0)
    lane_group = iota((8, LANES), 1) // 8
    own_group = lane_group == sub

    vals[...] = jnp.zeros_like(vals)
    vals[6:7, :] = jnp.full((1, wide), -1.0, F32)
    upper = jnp.where(iota((LANES, LANES), 0) <= iota((LANES, LANES), 1), 1.0, 0.0).astype(BF16)
    for load in loads[0:4]:
        load.wait()
    tile = tile_in[...]
    vals[6:7, 0:marks] = ((tile & YZ) + ((tile - q) & (YZ - 1))).astype(F32)
    vals[0:1, 0:marks] = site_in[...].reshape(1, marks).astype(F32)
    stiffness = stiff[...].reshape(1, marks)
    vals[1:2, 0:marks] = stiffness
    vals[2:5, 0:marks] = -stiffness * disp[...]
    tile8 = jnp.broadcast_to(vals[6:7, :].astype(I32), (8, wide))
    sub_wide = iota((8, wide), 0)
    member = [jnp.where(tile8 == sub_wide + 8 * half, 1.0, 0.0) for half in range(2)]
    member = jnp.concatenate(member, axis=0)
    stacked = jnp.concatenate([member[:, b * LANES : (b + 1) * LANES] for b in range(blocks)], axis=0)
    counts = product(stacked.astype(BF16), upper, False)
    offset = jnp.full((TILES, 1), -1.0, F32)
    ranks = []
    for b in range(blocks):
        count = counts[b * TILES : (b + 1) * TILES, :]
        mine = member[:, b * LANES : (b + 1) * LANES]
        ranks.append(jnp.sum(mine * (count + offset), axis=0, keepdims=True))
        offset = offset + count[:, LANES - 1 : LANES]
    rank8 = jnp.broadcast_to(jnp.concatenate(ranks, axis=1).astype(I32), (8, wide))
    for top in range(0, LANES, 16):
        pair = [jnp.where(sub_wide + (top + more) == rank8, 1.0, 0.0) for more in (0, 8)]
        hot[top : top + 16, :] = jnp.concatenate(pair, axis=0).astype(BF16)
    over = jnp.where(sub_wide + LANES == rank8, 1.0, 0.0)
    over = jnp.concatenate([over, over], axis=0).astype(BF16)
    for top in range(LANES, 2 * LANES, 16):
        hot[top : top + 16, :] = over

    value = jnp.where(sub_wide < 5, vals[...], 0.0)
    binned = None
    for part in parts_of(value, BIN_PARTS):
        left = jnp.concatenate([jnp.where(tile8 == k, part, 0.0) for k in range(TILES)], axis=0)
        term = product(left.astype(BF16), hot[...], True)
        binned = term if binned is None else binned + term
    for k in range(TILES):
        low_ranks = binned[k * 8 : (k + 1) * 8, 0:LANES]
        more = binned[k * 8 : (k + 1) * 8, LANES : 2 * LANES]
        more = jnp.sum(jnp.where(own_group, more, 0.0), axis=0, keepdims=True)
        payload[k] = jnp.where(sub == 5, more, low_ranks)

    pl.semaphore_wait(barrier, 2 * YZ - 1)

    def whole(buffer, sem):
        pltpu.make_async_copy(buffer, buffer, sem).wait()

    for half in (1, 0):
        for dq in far_first:
            k = half * YZ + dq
            if k != 0:
                pltpu.make_async_remote_copy(
                    src_ref=payload.at[k, pl.ds(0, PUT_ROWS)],
                    dst_ref=recv.at[k, pl.ds(0, PUT_ROWS)],
                    send_sem=put_send,
                    recv_sem=put_recv.at[half],
                    device_id=device(half, dq),
                    device_id_type=MESH,
                ).start()

    lane_rows = [(iota((16, LANES), 0) + top).astype(F32).astype(BF16) for top in range(0, 2 * LANES, 16)]
    one = jnp.ones((16, LANES), BF16)
    zero = jnp.zeros((16, LANES), BF16)

    def row_of(site):
        return ((site >> 7) & 31) ^ ((site >> 12) * 24)

    def packed(row):
        return jnp.broadcast_to(row, (16, LANES)).astype(BF16)


    def place_group(k, block):
        site = block[0:1, :].astype(I32)
        place = packed((((site >> 12) << 7) + (site & 127)).astype(F32))
        lanes = slice(k * LANES, (k + 1) * LANES)
        for number, index in enumerate(lane_rows):
            zhot[number * 16 : (number + 1) * 16, lanes] = jnp.where(index == place, one, zero)
        row = packed(row_of(site).astype(F32))
        masks = [lane_rows[number] == row for number in range(2)]
        for number, part in enumerate(parts_of(block, STEP_PARTS)):
            for c in range(4):
                top = (number * 4 + c) * 32
                value = packed(part[1 + c : 2 + c, :])
                for below, mask in enumerate(masks):
                    lhs[top + below * 16 : top + (below + 1) * 16, lanes] = jnp.where(mask, value, zero)

    tail = jnp.zeros((8, LANES), F32)
    for half in range(2):
        first = 1 if half == 0 else YZ
        whole(recv.at[pl.ds(first, (half + 1) * YZ - first), pl.ds(0, PUT_ROWS)], put_recv.at[half])
        for k in range(half * YZ, (half + 1) * YZ):
            block = payload[0] if k == 0 else recv[k]
            slots[k] = block
            more = jnp.where(own_group, jnp.broadcast_to(block[5:6, :], (8, LANES)), 0.0)
            tail = tail + jnp.where(lane_group == k, spread(more), 0.0)
            place_group(k, block)
        if half == 1:
            slots[TILES] = tail
            place_group(TILES, tail)
        lanes = slice(half * YZ * LANES, YZ * LANES if half == 0 else SLOTS)
        result = product(lhs[:, lanes], zhot[:, lanes], True)
        total = result[0:128, :]
        for number in range(1, STEP_PARTS):
            total = total + result[number * 128 : (number + 1) * 128, :]
        field[...] = total if half == 0 else field[...] + total
    for load in loads[4:]:
        load.wait()

    def streamed(index, main, skirt):
        _, cy, cz = lattice_dirs[index]
        value = main
        if cy != 0:
            value = jnp.where(sub == (7 if cy > 0 else 0), skirt, main)
            value = pltpu.roll(value, cy % 8, 0)
        if cz != 0:
            value = pltpu.roll(value, cz % LANES, 1)
        return value

    def remote(src, dst, send, recv_of, dg, dq):
        pltpu.make_async_remote_copy(
            src_ref=src,
            dst_ref=dst,
            send_sem=send,
            recv_sem=recv_of,
            device_id=device(dg, dq),
            device_id_type=MESH,
        ).start()

    def margin(channels, ax, ay, dg, dq, which):
        first, count = channels
        part = pl.ds(first, count)
        a_src, a_dst = {0: (2, 2), 1: (10 - ax, 2 - ax), -1: (2, 10)}[dg]
        slices = ax if dg != 0 else 8
        b_src = {0: 0, 1: 8 - ay, -1: 0}[dq]
        rows = pl.ds(b_src, ay if dq != 0 else 8)
        into = main if dq == 0 else skirt
        remote(
            main.at[part, pl.ds(a_src, slices), rows],
            into.at[part, pl.ds(a_dst, slices), rows],
            halo_send.at[0, which],
            halo_recv.at[0, which],
            dg,
            dq,
        )

    def margin_x():
        for dg, dq in ((1, 1), (-1, -1), (1, -1), (-1, 1)):
            margin(RUNS[dg, dq], 2, 2, dg, dq, 0)
            margin(RUNS[dg, 0], 2, 1, dg, dq, 0)
            margin(RUNS[0, dq], 1, 2, dg, dq, 0)
            margin(RUNS[0, 0], 1, 1, dg, dq, 0)
        for dg in (1, -1):
            margin((0 if dg > 0 else 18, 5), 2, 0, dg, 0, 0)
            margin((5, 13), 1, 0, dg, 0, 0)

    def margin_y():
        for dq in (1, -1):
            for cx in (1, 0, -1):
                margin(RUNS[cx, dq], 0, 2, 0, dq, 1)
                margin(RUNS[cx, 0], 0, 1, 0, dq, 1)

    def span(a):
        low = min(a, 7 - a) * 8
        high = (a // 4) * LANES
        return [(slice(c * 32 + low, c * 32 + low + 8), slice(high, high + LANES)) for c in range(4)]

    def first_step(a):
        spans = span(a)
        stiff_sum, *forces = [field[place] for place in spans]
        result, speed = collide([start[index, a] for index in range(19)], forces, solid[a])
        for index in range(19):
            main[SPOT[index], a + 2] = result[index]
        for c in range(3):
            usum[spans[c]] = speed[c]
            main[SPOT[19 + c], a + 2] = forces[c] - stiff_sum * speed[c]
        main[SPOT[22], a + 2] = solid[a].astype(F32)

    def second_step(a, outside):
        own, other = (skirt, main) if outside else (main, skirt)
        popul = []
        for index in range(19):
            source = a - lattice_dirs[index][0] + 2
            spot = SPOT[index]
            popul.append(streamed(index, own[spot, source], other[spot, source]))
        forces = [own[SPOT[19 + c], a + 2] for c in range(3)]
        result, speed = collide(popul, forces, own[SPOT[22], a + 2])
        for index in range(19):
            cx, cy, _ = lattice_dirs[index]
            enters = cx == 1 if a < 0 else cx == -1 if a > 7 else True
            if enters and (cy != 0 or not outside):
                (skirt_next if outside else main_next)[index, a + 1] = result[index]
        if not outside and 0 <= a < 8:
            spans = span(a)
            stiff_sum = field[spans[0]]
            for c in range(3):
                usum[spans[c]] = usum[spans[c]] + speed[c]
                field[spans[c + 1]] = forces[c] - stiff_sum * speed[c]

    def third_step(a):
        popul = []
        for index in range(19):
            source = a - lattice_dirs[index][0] + 1
            popul.append(streamed(index, main_next[index, source], skirt_next[index, source]))
        spans = span(a)
        result, speed = collide(popul, [field[place] for place in spans[1:]], solid[a])
        for c in range(3):
            usum[spans[c]] = usum[spans[c]] + speed[c]
        for index in range(19):
            post[index, a] = result[index]
        for side, edge in ((0, 7), (1, 0)):
            if a == edge:
                for place, index in enumerate(X_FACE[side]):
                    edges[5 * side + place] = result[index]
            for place, index in enumerate(Y_FACE[side]):
                edges[10 + 5 * side + place, a : a + 1, :] = result[index][edge : edge + 1, :]

    def halo(src, first, count, dg, dq):
        which = 0 if first < 14 else 1
        remote(
            edges.at[pl.ds(src, count)],
            halos.at[pl.ds(first, count)],
            halo_send.at[1, which],
            halo_recv.at[1, which],
            dg,
            dq,
        )

    def pulled(index, a):
        cx, cy, _ = lattice_dirs[index]
        x_side = 0 if cx > 0 else 1
        y_side = 0 if cy > 0 else 1
        source = a - cx
        inside = 0 <= source < 8
        value = post[index, source] if inside else halos[5 * x_side + X_FACE[x_side].index(index)]
        other = value
        if cy != 0:
            if inside:
                tile_of = 14 + 5 * y_side + Y_FACE[y_side].index(index)
                other = jnp.broadcast_to(halos[tile_of, source : source + 1, :], (8, LANES))
            else:
                other = halos[10 + CORNER.index(index)]
        return streamed(index, value, other)

    def gather():
        left = jnp.concatenate([part.astype(BF16) for part in parts_of(usum[...], STEP_PARTS)], axis=0)
        for k in range(GROUPS):
            if k % 2 == 0:
                picked = product(left, zhot[:, k * LANES : min(k + 2, GROUPS) * LANES], False)
                total = picked[0:96, :]
                for number in range(1, STEP_PARTS):
                    total = total + picked[number * 96 : (number + 1) * 96, :]
            mask = iota((32, LANES), 0) == row_of(slots[k][0:1, :].astype(I32))
            lanes = slice((k % 2) * LANES, (k % 2 + 1) * LANES)
            for c in range(3):
                speed = jnp.where(mask, total[c * 32 : (c + 1) * 32, lanes], 0.0)
                yield k, c, jnp.sum(speed, axis=0, keepdims=True)

    for a in (0, 1, 6, 7):
        first_step(a)
    margin_x()
    for a in range(2, 6):
        first_step(a)
    margin_y()
    whole(main.at[:, pl.ds(0, 2)], halo_recv.at[0, 1])
    for a in range(1, 7):
        second_step(a, False)
        second_step(a, True)
    for a in range(2, 6):
        third_step(a)
    whole(main.at[:, pl.ds(0, 5), pl.ds(0, 4)], halo_recv.at[0, 0])
    for a in (-1, 0, 7, 8):
        second_step(a, False)
        second_step(a, True)
    third_step(0)
    third_step(7)
    for number, index in enumerate(CORNER):
        cx, cy, _ = lattice_dirs[index]
        side = 0 if cx > 0 else 1
        halo(5 * side + X_FACE[side].index(index), 10 + number, 1, cx, cy)
    for side, dg in ((0, 1), (1, -1)):
        halo(5 * side, 5 * side, 5, dg, 0)
    third_step(1)
    third_step(6)
    for side, dq in ((0, 1), (1, -1)):
        halo(10 + 5 * side, 14 + 5 * side, 5, 0, dq)

    moved = []
    for k, c, speed in gather():
        if c == 0:
            moved.append(jnp.zeros((8, LANES), F32))
        moved[k] = jnp.where(sub == c, speed, moved[k])
    tail = moved[TILES]
    for half in (1, 0):
        for dq in far_first:
            k = half * YZ + dq
            more = spread(jnp.where(lane_group == k, tail, 0.0))
            more = jnp.sum(jnp.where(own_group, more, 0.0), axis=0, keepdims=True)
            block = jnp.where(sub == 3, more, moved[k])[0:4, :]
            if k == 0:
                ret[0] = block
            else:
                back[k] = block
                pltpu.make_async_remote_copy(
                    src_ref=back.at[k],
                    dst_ref=ret.at[k],
                    send_sem=ret_send,
                    recv_sem=ret_recv,
                    device_id=device(-half, -dq),
                    device_id_type=MESH,
                ).start()

    whole(halos.at[pl.ds(14, 10)], halo_recv.at[1, 1])
    for a in range(1, 7):
        for index in range(19):
            out_ref[index, a] = pulled(index, a)
    whole(halos.at[pl.ds(0, 14)], halo_recv.at[1, 0])
    for a in (0, 7):
        for index in range(19):
            out_ref[index, a] = pulled(index, a)
    whole(main.at[:, pl.ds(0, 5), pl.ds(0, 4)], halo_send.at[0, 0])
    whole(main.at[:, pl.ds(0, 2)], halo_send.at[0, 1])
    whole(halos.at[pl.ds(0, 14)], halo_send.at[1, 0])
    whole(halos.at[pl.ds(14, 10)], halo_send.at[1, 1])
    whole(recv.at[pl.ds(1, TILES - 1), pl.ds(0, PUT_ROWS)], put_send)

    whole(ret.at[pl.ds(1, TILES - 1)], ret_recv)
    own4 = own_group[0:4]
    lefts = []
    for k in range(TILES):
        block = ret[k]
        more = jnp.where(own4, jnp.broadcast_to(block[3:4, :], (4, LANES)), 0.0)
        lefts.append(jnp.concatenate([block, more], axis=1))
    left = jnp.concatenate(lefts, axis=0)
    left = jnp.concatenate([part.astype(BF16) for part in parts_of(left, BIN_PARTS)], axis=0)
    taken = product(left, hot[...], False)
    rows = 4 * TILES
    total = taken[0:rows, :]
    for number in range(1, BIN_PARTS):
        total = total + taken[number * rows : (number + 1) * rows, :]
    final = None
    tile8 = jnp.broadcast_to(vals[6:7, :].astype(I32), (8, wide)) - (sub_wide >> 2)
    for pair in range(YZ):
        term = jnp.where(tile8 == 2 * pair, total[pair * 8 : (pair + 1) * 8, :], 0.0)
        final = term if final is None else final + term
    final = final[0:4, :] + final[4:8, :]
    dout_ref[...] = disp[...] + final[0:3, 0:marks]
    whole(ret.at[pl.ds(1, TILES - 1)], ret_send)


def flush(pop_ref, disp_ref, pop_hbm, disp_hbm, sems):
    copies = [pltpu.make_async_copy(disp_ref, disp_hbm, sems.at[0])]
    step = 4
    for number, first in enumerate(range(0, pop_ref.shape[0], step)):
        part = pl.ds(first, min(step, pop_ref.shape[0] - first))
        copies.append(pltpu.make_async_copy(pop_ref.at[part], pop_hbm.at[part], sems.at[number + 1]))
    for copy in copies:
        copy.start()
    for copy in copies:
        copy.wait()


def body(populations, solid, displacement, stiffness, marker_tile, marker_site):
    marks = displacement.shape[1]
    wide = -(-marks // LANES) * LANES
    vmem = pl.BlockSpec(memory_space=pltpu.VMEM)
    hbm = pl.BlockSpec(memory_space=pltpu.HBM)
    dma = pltpu.SemaphoreType.DMA
    final_pop, final_disp = pl.pallas_call(
        kernel,
        out_shape=(
            jax.ShapeDtypeStruct(populations.shape, F32),
            jax.ShapeDtypeStruct(displacement.shape, F32),
        ),
        in_specs=[hbm] * 6,
        out_specs=(vmem, vmem),
        scratch_shapes=[
            pltpu.VMEM(populations.shape, F32),
            pltpu.VMEM(solid.shape, I32),
            pltpu.VMEM(displacement.shape, F32),
            pltpu.VMEM((marks,), F32),
            pltpu.VMEM((1, marks), I32),
            pltpu.VMEM((marks,), I32),
            pltpu.VMEM((8, wide), F32),
            pltpu.VMEM((2 * LANES, wide), BF16),
            pltpu.VMEM((TILES, 8, LANES), F32),
            pltpu.VMEM((TILES, 8, LANES), F32),
            pltpu.VMEM((2 * LANES, SLOTS), BF16),
            pltpu.VMEM((128 * STEP_PARTS, SLOTS), BF16),
            pltpu.VMEM((96, 2 * LANES), F32),
            pltpu.VMEM((128, 2 * LANES), F32),
            pltpu.VMEM((GROUPS, 8, LANES), F32),
            pltpu.VMEM((23, 12, 8, LANES), F32),
            pltpu.VMEM((23, 12, 8, LANES), F32),
            pltpu.VMEM((19, 10, 8, LANES), F32),
            pltpu.VMEM((19, 10, 8, LANES), F32),
            pltpu.VMEM(populations.shape, F32),
            pltpu.VMEM((20, 8, LANES), F32),
            pltpu.VMEM((24, 8, LANES), F32),
            pltpu.VMEM((TILES, 4, LANES), F32),
            pltpu.VMEM((TILES, 4, LANES), F32),
            dma((6,)),
            dma,
            dma((2,)),
            dma,
            dma,
            dma((2, 2)),
            dma((2, 2)),
        ],
        compiler_params=pltpu.CompilerParams(
            collective_id=0, has_side_effects=True, vmem_limit_bytes=16 * 1024 * 1024
        ),
        name="lattice_steps",
    )(
        *(
            pltpu.with_memory_space_constraint(value, pltpu.HBM)
            for value in (
                populations,
                solid,
                displacement,
                stiffness,
                marker_tile.reshape(1, -1),
                marker_site,
            )
        )
    )
    return pl.pallas_call(
        flush,
        out_shape=(
            jax.ShapeDtypeStruct(populations.shape, F32),
            jax.ShapeDtypeStruct(displacement.shape, F32),
        ),
        in_specs=[vmem, vmem],
        out_specs=(hbm, hbm),
        scratch_shapes=[dma((6,))],
        compiler_params=pltpu.CompilerParams(vmem_limit_bytes=16 * 1024 * 1024),
        name="write_out",
    )(final_pop, final_disp)


def solution(mesh):
    in_specs = (
        P(None, "gx", "yz", None),
        P("gx", "yz", None),
        P(None, ("gx", "yz")),
        P(("gx", "yz")),
        P(("gx", "yz"), None),
        P(("gx", "yz")),
    )
    out_specs = (P(None, "gx", "yz", None), P(None, ("gx", "yz")))
    return jax.shard_map(body, mesh=mesh, in_specs=in_specs, out_specs=out_specs, check_vma=False)
```
